256 devices in a mesh: subj: 16 (over z, core), vox: 16 (over y, x).
Axes of the slice: x: 4, y: 4, z: 8, core: 2. Of those that a mesh axis runs over, the one named last changes fastest.
Arguments:
- data: bfloat16 [32, 240, 65536], P('subj', None, 'vox'), may hold values from -40 to 40, as said below
- shared_start: bfloat16 [128, 240], replicated, may hold values from -6 to 6
Outputs:
- projections: float32 [32, 128, 240], P('subj')
- response: float32 [128, 240], replicated
The draws below stay inside these ranges and needn't reach their ends.
Inputs may be any that keep to these rules, and one draw needn't show every extreme that they name: `data`: real-valued recordings.
All inputs are finite; a program needn't handle non-finite values.
Results may differ from the reference program's by a relative error of at most 0.00035.
The reference program's roundings to bfloat16 on the way (of `shared`) count: a program that leaves them out, or rounds other values in their place, can miss the bound.
Values may be sent and summed in bfloat16 or wider, within the bound.
No kernel may reach another device: no remote copies, remote signals or barrier semaphores. Data moves between devices by JAX's collectives and lax.ppermute only.
A program may use at most 64 MiB of HBM per device.

```python
import jax
import jax.numpy as jnp
from jax import lax

FEATURES = 128
FRAMES = 240
ITERS = 3
OUTER = 2
SUBJECTS = 32
VOXELS = 65536


def draw_data(key, part):
    first, second, third = jax.random.split(jax.random.fold_in(key, 11), 3)
    voxel_scale = 10.0 ** (jax.random.uniform(second, (SUBJECTS, 1, VOXELS), jnp.float32) - 0.5)
    frame_scale = 10.0 ** (jax.random.uniform(third, (SUBJECTS, FRAMES, 1), jnp.float32) - 0.5)
    base = jnp.clip(jax.random.normal(first, (SUBJECTS, FRAMES, VOXELS), jnp.float32), -4.0, 4.0)
    return (base * voxel_scale * frame_scale).astype(jnp.bfloat16)


def noise(own_key, dims, spread, bound, dtype=jnp.bfloat16):
    drawn = jax.random.normal(own_key, dims, jnp.float32) * spread
    return jnp.minimum(jnp.maximum(drawn, -bound), bound).astype(dtype)


def setup_inputs(seed: int = 0) -> dict:
    streams_of = jax.random.split(jax.random.key(seed), 3)
    return {
        "data": draw_data(jax.random.fold_in(streams_of[2], 71), 0),
        "shared_start": noise(streams_of[1], (FEATURES, FRAMES), 1.0, 6.0),
    }


def refit(record, shared):
    cross = jnp.dot(record.T, shared.T, preferred_element_type=jnp.float32)
    scale = jnp.sqrt(jnp.sum(cross * cross) + 1e-06)
    iterate = cross / scale
    for count in range(ITERS):
        gram = jnp.dot(iterate.T, iterate, precision=lax.Precision.HIGHEST)
        iterate = 1.5 * iterate - 0.5 * jnp.dot(iterate, gram, precision=lax.Precision.HIGHEST)
    return jnp.dot(iterate.T, record.T.astype(jnp.float32), precision=lax.Precision.HIGHEST)

def reference(data, shared_start):
    shared = shared_start
    projections = None
    response = None
    for outer in range(OUTER):
        projections = lax.map(lambda record: refit(record, shared), data)
        response = lax.optimization_barrier(jnp.sum(projections, axis=0)) / jnp.float32(SUBJECTS)
        shared = response.astype(jnp.bfloat16)
    return (projections, response)
```

```python
import jax
import jax.numpy as jnp
from jax import lax
from jax.experimental import pallas as pl
from jax.experimental.pallas import tpu as pltpu
from jax.sharding import PartitionSpec as P

ITERS = 3
OUTER = 2
LANES = 128
HIGHEST = lax.Precision.HIGHEST


def padded(frames):
    return -(-frames // (2 * LANES)) * 2 * LANES


def positions(size):
    rows = lax.broadcasted_iota(jnp.int32, (size, size), 0)
    cols = lax.broadcasted_iota(jnp.int32, (size, size), 1)
    return rows, cols


def gram_kernel(data_ref, packed_ref, sums_ref):
    step = pl.program_id(0)
    frames = data_ref.shape[1]
    size = packed_ref.shape[1]

    @pl.when(step == 0)
    def _():
        sums_ref[...] = jnp.zeros_like(sums_ref)

    for subject in range(2):
        block = data_ref[subject]
        sums_ref[subject] += lax.dot_general(
            block, block, (((1,), (1,)), ((), ())), preferred_element_type=jnp.float32
        )

    @pl.when(step == pl.num_programs(0) - 1)
    def _():
        rows, cols = positions(frames)
        first, second = sums_ref[0], sums_ref[1]
        mixed = jnp.where(rows >= cols, first, second)
        diagonal = jnp.sum(jnp.where(rows == cols, second, 0.0), axis=1, keepdims=True)
        packed_ref[...] = jnp.zeros_like(packed_ref)
        packed_ref[0:frames, 0:frames] = mixed
        packed_ref[0:frames, frames : frames + 1] = diagonal


def packed_grams(data, size):
    subjects, frames, voxels = data.shape
    tile = 1024
    return pl.pallas_call(
        gram_kernel,
        grid=(voxels // tile,),
        in_specs=[pl.BlockSpec((subjects, frames, tile), lambda i: (0, 0, i))],
        out_specs=pl.BlockSpec((size, size), lambda i: (0, 0)),
        out_shape=jax.ShapeDtypeStruct((size, size), jnp.float32),
        scratch_shapes=[pltpu.VMEM((subjects, frames, frames), jnp.float32)],
        name="grams",
    )(data)


def in_three(x):
    high = x.astype(jnp.bfloat16)
    rest = x - high.astype(jnp.float32)
    middle = rest.astype(jnp.bfloat16)
    low = (rest - middle.astype(jnp.float32)).astype(jnp.bfloat16)
    return high, middle, low


def exact_right(x, y, dims):
    return sum(
        lax.dot_general(part, y, (dims, ((), ())), preferred_element_type=jnp.float32)
        for part in in_three(x)
    )


def exact_left(x, y, dims):
    return sum(
        lax.dot_general(x, part, (dims, ((), ())), preferred_element_type=jnp.float32)
        for part in in_three(y)
    )


def times(a, b):
    return jnp.dot(a, b, precision=HIGHEST, preferred_element_type=jnp.float32)


def refit(gram, shared):
    crossed = exact_right(gram, shared, ((1,), (0,)))
    first = exact_left(shared, crossed, ((0,), (0,)))
    features = first.shape[0]
    rows, cols = positions(features)
    eye = (rows == cols).astype(jnp.float32)
    square = jnp.sum(first * eye) + 1e-06
    current = first / square
    result = crossed / jnp.sqrt(square)
    for count in range(ITERS):
        step = 1.5 * eye - 0.5 * current
        result = times(result, step)
        if count < ITERS - 1:
            current = times(times(current, step), step)
    return result


def refit_body(frames, last, place_ref, packed_ref, shared_ref, share_ref, *refs):
    total_ref, wide_ref = refs[-2:]
    size = packed_ref.shape[0]
    rows, cols = positions(size)
    packed = packed_ref[...]
    diagonal = packed[:, frames : frames + 1]
    packed = jnp.where(cols < frames, packed, 0.0)
    flipped = packed.T
    grams = (
        jnp.where(rows >= cols, packed, flipped),
        jnp.where(rows == cols, diagonal, jnp.where(rows < cols, packed, flipped)),
    )
    wide_ref[...] = jnp.zeros_like(wide_ref)
    wide_ref[0:frames, :] = shared_ref[0:frames, :]
    shared = wide_ref[...]
    results = [refit(gram, shared) for gram in grams]
    if last:
        for subject in range(2):
            refs[0][subject] = results[subject][0:frames, :]
    total_ref[...] = results[0] + results[1]
    width = share_ref.shape[1]
    share = total_ref[pl.ds(pl.multiple_of(place_ref[0] * width, width), width), :]
    for peer in range(share_ref.shape[0]):
        share_ref[peer] = share


def refits(packed, shared, place, frames, peers, last):
    size = packed.shape[0]
    features = shared.shape[1]
    width = size // peers
    out = [jax.ShapeDtypeStruct((peers, width, features), jnp.float32)]
    if last:
        out.append(jax.ShapeDtypeStruct((2, frames, features), jnp.float32))

    def kernel(*refs):
        return refit_body(frames, last, *refs)

    return pl.pallas_call(
        kernel,
        in_specs=[
            pl.BlockSpec(memory_space=pltpu.SMEM),
            pl.BlockSpec(memory_space=pltpu.VMEM),
            pl.BlockSpec(memory_space=pltpu.VMEM),
        ],
        out_specs=[pl.BlockSpec(memory_space=pltpu.VMEM)] * len(out),
        out_shape=out,
        scratch_shapes=[
            pltpu.VMEM((size, features), jnp.float32),
            pltpu.VMEM((size, features), jnp.bfloat16),
        ],
        name="refits_last" if last else "refits",
    )(place, packed, shared)


def exchanged(pieces, axis):
    return lax.all_to_all(pieces, axis, 0, 0, tiled=True)


def to_everyone(shard, peers):
    return jnp.broadcast_to(shard[None], (peers, *shard.shape))


def local(data, shared_start):
    frames = data.shape[1]
    peers = lax.axis_size("vox")
    subjects = data.shape[0] * lax.axis_size("subj")
    size = padded(frames)
    place = lax.axis_index("vox").astype(jnp.int32).reshape(1)
    pieces = packed_grams(data, size).reshape(peers, size // peers, size)
    share = jnp.sum(exchanged(pieces, "vox"), axis=0)
    packed = exchanged(to_everyone(share, peers), "vox").reshape(size, size)
    shared = shared_start.T
    for outer in range(OUTER):
        last = outer == OUTER - 1
        out = refits(packed, shared, place, frames, peers, last)
        total = jnp.sum(exchanged(out[0], "subj"), axis=0) / jnp.float32(subjects)
        if not last:
            total = total.astype(jnp.bfloat16)
        shared = exchanged(to_everyone(total, peers), "vox").reshape(size, -1)
    projections = jnp.swapaxes(out[1], 1, 2)
    return (projections, shared[:frames].T)


def solution(mesh):
    placed = (P("subj", None, "vox"), P())
    return jax.shard_map(
        local, mesh=mesh, in_specs=placed, out_specs=(P("subj", None, None), P()), check_vma=False
    )
```

```python
import jax
import jax.numpy as jnp
from jax import lax
from jax.experimental import pallas as pl
from jax.experimental.pallas import tpu as pltpu
from jax.sharding import PartitionSpec as P

ITERS = 3
OUTER = 2
LANES = 128
VMEM = pl.BlockSpec(memory_space=pltpu.VMEM)
SMEM = pl.BlockSpec(memory_space=pltpu.SMEM)


def padded(frames):
    return -(-frames // (2 * LANES)) * 2 * LANES


def positions(size):
    rows = lax.broadcasted_iota(jnp.int32, (size, size), 0)
    cols = lax.broadcasted_iota(jnp.int32, (size, size), 1)
    return rows, cols


def gram_kernel(data_ref, start_ref, packed_ref, shared_ref, sums_ref):
    step = pl.program_id(0)
    frames = data_ref.shape[1]

    @pl.when(step == 0)
    def _():
        sums_ref[...] = jnp.zeros_like(sums_ref)
        shared_ref[...] = jnp.zeros_like(shared_ref)
        shared_ref[:, 0:frames] = start_ref[...].T

    for subject in range(2):
        block = data_ref[subject]
        sums_ref[subject] += lax.dot_general(
            block, block, (((1,), (1,)), ((), ())), preferred_element_type=jnp.float32
        )

    @pl.when(step == pl.num_programs(0) - 1)
    def _():
        rows, cols = positions(frames)
        first, second = sums_ref[0], sums_ref[1]
        mixed = jnp.where(rows >= cols, first, second)
        diagonal = jnp.sum(jnp.where(rows == cols, second, 0.0), axis=1, keepdims=True)
        packed_ref[...] = jnp.zeros_like(packed_ref)
        packed_ref[0:frames, 0:frames] = mixed
        packed_ref[0:frames, frames : frames + 1] = diagonal


def packed_grams(data, start, size):
    subjects, frames, voxels = data.shape
    features = start.shape[1]
    tile = 1024
    return pl.pallas_call(
        gram_kernel,
        grid=(voxels // tile,),
        in_specs=[pl.BlockSpec((subjects, frames, tile), lambda i: (0, 0, i)), VMEM],
        out_specs=[VMEM, VMEM],
        out_shape=[
            pltpu.VMEM((size, size), jnp.float32),
            pltpu.VMEM((features, size), jnp.bfloat16),
        ],
        scratch_shapes=[pltpu.VMEM((subjects, frames, frames), jnp.float32)],
        name="grams",
    )(data, start)


def parts_of(x, count):
    parts = []
    for part in range(count):
        parts.append(x.astype(jnp.bfloat16))
        if part < count - 1:
            x = x - parts[-1].astype(jnp.float32)
    return parts


def product(a, b, dims=((1,), (0,))):
    return lax.dot_general(a, b, (dims, ((), ())), preferred_element_type=jnp.float32)


def times(a, b):
    width = b.shape[1]
    a_both = jnp.concatenate(parts_of(a, 2), axis=1)
    high, low = parts_of(b, 2)
    if 2 * width <= 2 * LANES:
        wide = jnp.concatenate([high, low], axis=1)
        out = product(a_both, jnp.concatenate([wide, wide], axis=0))
        return out[:, :width] + out[:, width:]
    out = product(a_both, jnp.concatenate([high, high], axis=0))
    return out + product(a_both, jnp.concatenate([low, low], axis=0))


def refit(gram, shared, count):
    crossed = sum(product(shared, part) for part in parts_of(gram, count))
    square = jnp.sum(crossed * shared.astype(jnp.float32)) + 1e-06
    first = sum(product(shared, part, ((1,), (1,))) for part in parts_of(crossed, count))
    current = first * (1.0 / square)
    result = crossed * (1.0 / jnp.sqrt(square))
    for step in range(ITERS):
        if step < ITERS - 1:
            half = 1.5 * current - 0.5 * times(current, current)
        result = 1.5 * result - 0.5 * times(current, result)
        if step < ITERS - 1:
            current = 1.5 * half - 0.5 * times(half, current)
    return result


def refit_kernel(frames, last, place_ref, packed_ref, shared_ref, share_ref, *refs):
    total_ref = refs[-1]
    size = total_ref.shape[1]
    rows, cols = positions(size)
    packed = packed_ref[...]
    diagonal = packed[:, frames : frames + 1]
    packed = jnp.where(cols < frames, packed, 0.0)
    flipped = packed.T
    grams = (
        jnp.where(rows >= cols, packed, flipped),
        jnp.where(rows == cols, diagonal, jnp.where(rows < cols, packed, flipped)),
    )
    shared = shared_ref[...]
    results = [refit(gram, shared, 2 if last else 3) for gram in grams]
    if last:
        for subject in range(2):
            refs[0][subject] = results[subject]
    total_ref[...] = results[0] + results[1]
    width = share_ref.shape[1]
    share = total_ref[pl.ds(pl.multiple_of(place_ref[0] * width, width), width), :]
    for peer in range(share_ref.shape[0]):
        share_ref[peer] = share


def refits(packed, shared, place, frames, peers, last):
    features, size = shared.shape
    out = [pltpu.VMEM((peers, features // peers, size), jnp.float32)]
    if last:
        out.append(pltpu.VMEM((2, features, size), jnp.float32))

    def kernel(*refs):
        return refit_kernel(frames, last, *refs)

    return pl.pallas_call(
        kernel,
        in_specs=[SMEM, VMEM, VMEM],
        out_specs=[VMEM] * len(out),
        out_shape=out,
        scratch_shapes=[pltpu.VMEM((features, size), jnp.float32)],
        name="refits_last" if last else "refits",
    )(place, in_vmem(packed), in_vmem(shared))


def in_vmem(x):
    return pltpu.with_memory_space_constraint(x, pltpu.VMEM)


def exchanged(pieces, axis):
    return lax.all_to_all(pieces, axis, 0, 0, tiled=True)


def to_everyone(shard, peers):
    return jnp.broadcast_to(shard[None], (peers, *shard.shape))


def local(data, shared_start):
    frames = data.shape[1]
    peers = lax.axis_size("vox")
    subjects = data.shape[0] * lax.axis_size("subj")
    size = padded(frames)
    place = lax.axis_index("vox").astype(jnp.int32).reshape(1)
    packed, shared = packed_grams(data, shared_start.T, size)
    packed, place = lax.optimization_barrier((packed, place))
    share = jnp.sum(exchanged(packed.reshape(peers, size // peers, size), "vox"), axis=0)
    packed = exchanged(to_everyone(share, peers), "vox").reshape(size, size)
    for outer in range(OUTER):
        last = outer == OUTER - 1
        out = refits(packed, shared, place, frames, peers, last)
        total = jnp.sum(exchanged(out[0], "subj"), axis=0) / jnp.float32(subjects)
        if not last:
            total = total.astype(jnp.bfloat16)
        shared = exchanged(to_everyone(total, peers), "vox").reshape(-1, size)
    return (out[1][:, :, :frames], shared[:, :frames])


def solution(mesh):
    placed = (P("subj", None, "vox"), P())
    return jax.shard_map(
        local, mesh=mesh, in_specs=placed, out_specs=(P("subj", None, None), P()), check_vma=False
    )
```

```python
import jax
import jax.numpy as jnp
from jax import lax
from jax.experimental import pallas as pl
from jax.experimental.pallas import tpu as pltpu
from jax.sharding import Mesh, PartitionSpec as P

ITERS = 3
LANES = 128
VMEM = pl.BlockSpec(memory_space=pltpu.VMEM)
SMEM = pl.BlockSpec(memory_space=pltpu.SMEM)


def padded(frames):
    return -(-frames // (2 * LANES)) * 2 * LANES


def positions(size):
    rows = lax.broadcasted_iota(jnp.int32, (size, size), 0)
    cols = lax.broadcasted_iota(jnp.int32, (size, size), 1)
    return rows, cols


def gram_kernel(data_ref, start_ref, packed_ref, shared_ref, sums_ref):
    step = pl.program_id(0)
    frames = data_ref.shape[1]

    @pl.when(step == 0)
    def _():
        sums_ref[...] = jnp.zeros_like(sums_ref)
        shared_ref[...] = jnp.zeros_like(shared_ref)
        shared_ref[:, 0:frames] = start_ref[...].T

    for subject in range(2):
        block = data_ref[subject]
        sums_ref[subject] += lax.dot_general(
            block, block, (((1,), (1,)), ((), ())), preferred_element_type=jnp.float32
        )

    @pl.when(step == pl.num_programs(0) - 1)
    def _():
        rows, cols = positions(frames)
        first, second = sums_ref[0], sums_ref[1]
        mixed = jnp.where(rows >= cols, first, second)
        diagonal = jnp.sum(jnp.where(rows == cols, second, 0.0), axis=1, keepdims=True)
        packed_ref[...] = jnp.zeros_like(packed_ref)
        packed_ref[0:frames, 0:frames] = mixed
        packed_ref[0:frames, frames : frames + 1] = diagonal


def packed_grams(data, start, size):
    subjects, frames, voxels = data.shape
    features = start.shape[1]
    tile = 2048
    return pl.pallas_call(
        gram_kernel,
        grid=(voxels // tile,),
        in_specs=[pl.BlockSpec((subjects, frames, tile), lambda i: (0, 0, i)), VMEM],
        out_specs=[VMEM, VMEM],
        out_shape=[
            pltpu.VMEM((size, size), jnp.float32),
            pltpu.VMEM((features, size), jnp.bfloat16),
        ],
        scratch_shapes=[pltpu.VMEM((subjects, frames, frames), jnp.float32)],
        name="grams",
    )(data, start)


def parts_of(x, count):
    parts = []
    for part in range(count):
        parts.append(x.astype(jnp.bfloat16))
        if part < count - 1:
            x = x - parts[-1].astype(jnp.float32)
    return parts


def product(a, b, dims=((1,), (0,))):
    return lax.dot_general(a, b, (dims, ((), ())), preferred_element_type=jnp.float32)


def times(a, b):
    width = b.shape[1]
    a_both = jnp.concatenate(parts_of(a, 2), axis=1)
    high, low = parts_of(b, 2)
    if 2 * width <= 2 * LANES:
        wide = jnp.concatenate([high, low], axis=1)
        out = product(a_both, jnp.concatenate([wide, wide], axis=0))
        return out[:, :width] + out[:, width:]
    out = product(a_both, jnp.concatenate([high, high], axis=0))
    return out + product(a_both, jnp.concatenate([low, low], axis=0))


def refit(gram, shared, count):
    crossed = sum(product(shared, part) for part in parts_of(gram, count))
    square = jnp.sum(crossed * shared.astype(jnp.float32)) + 1e-06
    first = sum(product(shared, part, ((1,), (1,))) for part in parts_of(crossed, count))
    current = first * (1.0 / square)
    result = crossed * (1.0 / jnp.sqrt(square))
    for step in range(ITERS):
        if step < ITERS - 1:
            half = 1.5 * current - 0.5 * times(current, current)
        result = 1.5 * result - 0.5 * times(current, result)
        if step < ITERS - 1:
            current = 1.5 * half - 0.5 * times(half, current)
    return result


def refit_kernel(frames, last, place_ref, packed_ref, *refs):
    shared_refs, refs = refs[: 1 if not last else 4], refs[1 if not last else 4 :]
    keep_ref, give_ref, total_ref = refs[0], refs[1], refs[-1]
    size = total_ref.shape[1]
    width = keep_ref.shape[0]
    rows, cols = positions(size)
    packed = packed_ref[...]
    diagonal = packed[:, frames : frames + 1]
    packed = jnp.where(cols < frames, packed, 0.0)
    flipped = packed.T
    grams = (
        jnp.where(rows >= cols, packed, flipped),
        jnp.where(rows == cols, diagonal, jnp.where(rows < cols, packed, flipped)),
    )
    if last:
        shared_ref = refs[-2]
        for piece, piece_ref in enumerate(shared_refs):
            shared_ref[block(place_ref, piece, width), :] = piece_ref[...]
        shared = shared_ref[...]
    else:
        shared = shared_refs[0][...]
    results = [refit(gram, shared, 2 if last else 3) for gram in grams]
    if last:
        for subject in range(2):
            refs[2][subject] = results[subject]
    total_ref[...] = results[0] + results[1]
    keep_ref[...] = total_ref[block(place_ref, 0, width), :]
    give_ref[...] = total_ref[block(place_ref, 1, width), :]


def block(place_ref, piece, width):
    return pl.ds(pl.multiple_of(place_ref[piece] * width, width), width)


def refits(packed, shared, place, frames, features, last):
    size = packed.shape[1]
    quarter = pltpu.VMEM((features // 4, size), jnp.float32)
    out = [quarter, quarter]
    scratch = [pltpu.VMEM((features, size), jnp.float32)]
    if last:
        out.append(pltpu.VMEM((2, features, size), jnp.float32))
        scratch.insert(0, pltpu.VMEM((features, size), jnp.bfloat16))

    def kernel(*refs):
        return refit_kernel(frames, last, *refs)

    return pl.pallas_call(
        kernel,
        in_specs=[SMEM] + [VMEM] * (1 + len(shared)),
        out_specs=[VMEM] * len(out),
        out_shape=out,
        scratch_shapes=scratch,
        name="refits_last" if last else "refits",
    )(place, *(in_vmem(x) for x in (packed, *shared)))


def whole_kernel(place_ref, *refs):
    pieces, out_ref, whole_ref = refs[:4], refs[4], refs[5]
    for piece, piece_ref in enumerate(pieces):
        whole_ref[block(place_ref, piece, piece_ref.shape[0]), :] = piece_ref[...]
    out_ref[...] = whole_ref[...].T[0 : out_ref.shape[0], :]


def whole(pieces, place, frames):
    width, size = pieces[0].shape
    return pl.pallas_call(
        whole_kernel,
        in_specs=[SMEM] + [VMEM] * 4,
        out_specs=VMEM,
        out_shape=jax.ShapeDtypeStruct((frames, 4 * width), jnp.float32),
        scratch_shapes=[pltpu.VMEM((4 * width, size), jnp.float32)],
        name="whole",
    )(place, *(in_vmem(x) for x in pieces))


def in_vmem(x):
    return pltpu.with_memory_space_constraint(x, pltpu.VMEM)


def exchanged(pieces, axis):
    return lax.all_to_all(pieces, axis, 0, 0, tiled=True)


def to_everyone(shard, peers):
    return jnp.broadcast_to(shard[None], (peers, *shard.shape))


def swapped(x, core, across):
    cores, chips = lax.axis_size("core"), lax.axis_size("x")
    pairs = []
    for c in range(cores):
        for i in range(chips):
            to = (c ^ core) * chips + (i ^ across)
            pairs.append((c * chips + i, to))
    return lax.ppermute(x, ("core", "x"), pairs)


def all_summed(keep, give, dtype, scale, held=None):
    chip = keep + swapped(give, 1, 0)
    pieces = exchanged(to_everyone(chip, lax.axis_size("z")), "z")
    total = (jnp.sum(pieces, axis=0) * scale).astype(dtype)
    if held is not None:
        total, held = lax.optimization_barrier((total, held))
    return (total, swapped(total, 1, 0), swapped(total, 0, 1), swapped(total, 1, 1)), held


def local(data, shared_start):
    frames = data.shape[1]
    features = shared_start.shape[0]
    peers = lax.axis_size(("y", "x"))
    subjects = data.shape[0] * lax.axis_size(("z", "core"))
    size = padded(frames)
    core = lax.axis_index("core").astype(jnp.int32)
    side = 2 * (lax.axis_index("x").astype(jnp.int32) % 2)
    place = jnp.stack([side + core, side + 1 - core, 2 - side + core, 3 - side - core])
    packed, shared = packed_grams(data, shared_start.T, size)
    packed, place = lax.optimization_barrier((packed, place))
    share = jnp.sum(exchanged(packed.reshape(peers, size // peers, size), ("y", "x")), axis=0)
    packed = exchanged(to_everyone(share, peers), ("y", "x")).reshape(size, size)
    keep, give = refits(packed, (shared,), place, frames, features, False)
    pieces, _ = all_summed(keep, give, jnp.bfloat16, 1.0 / subjects)
    keep, give, projections = refits(packed, pieces, place, frames, features, True)
    pieces, projections = all_summed(keep, give, jnp.float32, 1.0 / subjects, projections)
    response = whole(pieces, place, frames)
    return (projections[:, :, :frames], response.T)


def solution(mesh):
    sizes = dict(mesh.shape)
    cores, across = 2, 4
    shape = (sizes["subj"] // cores, cores, sizes["vox"] // across, across)
    chips = Mesh(mesh.devices.reshape(shape), ("z", "core", "y", "x"))
    placed = (P(("z", "core"), None, ("y", "x")), P())
    return jax.shard_map(
        local,
        mesh=chips,
        in_specs=placed,
        out_specs=(P(("z", "core"), None, None), P()),
        check_vma=False,
    )
```

```python
import jax
import jax.numpy as jnp
from jax import lax
from jax.experimental import pallas as pl
from jax.experimental.pallas import tpu as pltpu
from jax.sharding import Mesh, PartitionSpec as P

ITERS = 3
LANES = 128
VMEM = pl.BlockSpec(memory_space=pltpu.VMEM)


def padded(frames):
    return -(-frames // (2 * LANES)) * 2 * LANES


def positions(size):
    rows = lax.broadcasted_iota(jnp.int32, (size, size), 0)
    cols = lax.broadcasted_iota(jnp.int32, (size, size), 1)
    return rows, cols


def gram_kernel(data_ref, start_ref, packed_ref, shared_ref, sums_ref):
    step = pl.program_id(0)
    frames = data_ref.shape[1]

    @pl.when(step == 0)
    def _():
        sums_ref[...] = jnp.zeros_like(sums_ref)
        shared_ref[...] = jnp.zeros_like(shared_ref)
        shared_ref[:, 0:frames] = start_ref[...].T

    for subject in range(2):
        block = data_ref[subject]
        sums_ref[subject] += lax.dot_general(
            block, block, (((1,), (1,)), ((), ())), preferred_element_type=jnp.float32
        )

    @pl.when(step == pl.num_programs(0) - 1)
    def _():
        rows, cols = positions(frames)
        first, second = sums_ref[0], sums_ref[1]
        mixed = jnp.where(rows >= cols, first, second)
        diagonal = jnp.sum(jnp.where(rows == cols, second, 0.0), axis=1, keepdims=True)
        packed_ref[...] = jnp.zeros_like(packed_ref)
        packed_ref[0:frames, 0:frames] = mixed
        packed_ref[0:frames, frames : frames + 1] = diagonal


def packed_grams(data, start, size):
    subjects, frames, voxels = data.shape
    features = start.shape[1]
    tile = 2048
    return pl.pallas_call(
        gram_kernel,
        grid=(voxels // tile,),
        in_specs=[pl.BlockSpec((subjects, frames, tile), lambda i: (0, 0, i)), VMEM],
        out_specs=[VMEM, VMEM],
        out_shape=[
            pltpu.VMEM((size, size), jnp.float32),
            pltpu.VMEM((features, size), jnp.bfloat16),
        ],
        scratch_shapes=[pltpu.VMEM((subjects, frames, frames), jnp.float32)],
        name="grams",
    )(data, start)


def parts_of(x, count):
    parts = []
    for part in range(count):
        parts.append(x.astype(jnp.bfloat16))
        if part < count - 1:
            x = x - parts[-1].astype(jnp.float32)
    return parts


def product(a, b, dims=((1,), (0,))):
    return lax.dot_general(a, b, (dims, ((), ())), preferred_element_type=jnp.float32)


def times(a, b):
    width = b.shape[1]
    a_both = jnp.concatenate(parts_of(a, 2), axis=1)
    high, low = parts_of(b, 2)
    if 2 * width <= 2 * LANES:
        wide = jnp.concatenate([high, low], axis=1)
        out = product(a_both, jnp.concatenate([wide, wide], axis=0))
        return out[:, :width] + out[:, width:]
    out = product(a_both, jnp.concatenate([high, high], axis=0))
    return out + product(a_both, jnp.concatenate([low, low], axis=0))


def refit(gram, shared, count):
    crossed = sum(product(shared, part) for part in parts_of(gram, count))
    square = jnp.sum(crossed * shared.astype(jnp.float32)) + 1e-06
    first = sum(product(shared, part, ((1,), (1,))) for part in parts_of(crossed, count))
    current = first * (1.0 / square)
    result = crossed * (1.0 / jnp.sqrt(square))
    for step in range(ITERS):
        if step < ITERS - 1:
            half = 1.5 * current - 0.5 * times(current, current)
        result = 1.5 * result - 0.5 * times(current, result)
        if step < ITERS - 1:
            current = 1.5 * half - 0.5 * times(half, current)
    return result


def refit_kernel(frames, last, packed_ref, *refs):
    shared_refs, refs = refs[: 1 if not last else 4], refs[1 if not last else 4 :]
    keep_ref, give_ref, total_ref = refs[0], refs[1], refs[-1]
    size = total_ref.shape[1]
    width = keep_ref.shape[0]
    rows, cols = positions(size)
    packed = packed_ref[...]
    diagonal = packed[:, frames : frames + 1]
    packed = jnp.where(cols < frames, packed, 0.0)
    flipped = packed.T
    grams = (
        jnp.where(rows >= cols, packed, flipped),
        jnp.where(rows == cols, diagonal, jnp.where(rows < cols, packed, flipped)),
    )
    if last:
        shared_ref = refs[-2]
        for piece, piece_ref in enumerate(shared_refs):
            shared_ref[block(piece, width), :] = piece_ref[...]
        shared = shared_ref[...]
    else:
        shared = shared_refs[0][...]
    results = [refit(gram, shared, 2 if last else 3) for gram in grams]
    if last:
        for subject in range(2):
            refs[2][subject] = results[subject]
    total_ref[...] = results[0] + results[1]
    keep_ref[...] = total_ref[block(0, width), :]
    give_ref[...] = total_ref[block(1, width), :]


def block(piece, width):
    core, side = lax.axis_index("core"), lax.axis_index("x") % 2
    core = 1 - core if piece % 2 else core
    side = 1 - side if piece // 2 else side
    return pl.ds(pl.multiple_of((2 * side + core) * width, width), width)


def refits(packed, shared, frames, features, last):
    size = packed.shape[1]
    quarter = pltpu.VMEM((features // 4, size), jnp.float32)
    out = [quarter, quarter]
    scratch = [pltpu.VMEM((features, size), jnp.float32)]
    if last:
        out.append(pltpu.VMEM((2, features, size), jnp.float32))
        scratch.insert(0, pltpu.VMEM((features, size), jnp.bfloat16))

    def kernel(*refs):
        return refit_kernel(frames, last, *refs)

    return pl.pallas_call(
        kernel,
        in_specs=[VMEM] * (1 + len(shared)),
        out_specs=[VMEM] * len(out),
        out_shape=out,
        scratch_shapes=scratch,
        name="refits_last" if last else "refits",
    )(*(in_vmem(x) for x in (packed, *shared)))


def whole_kernel(*refs):
    pieces, out_ref, whole_ref = refs[:4], refs[4], refs[5]
    for piece, piece_ref in enumerate(pieces):
        whole_ref[block(piece, piece_ref.shape[0]), :] = piece_ref[...]
    out_ref[...] = whole_ref[...].T[0 : out_ref.shape[0], :]


def whole(pieces, frames):
    width, size = pieces[0].shape
    return pl.pallas_call(
        whole_kernel,
        in_specs=[VMEM] * 4,
        out_specs=VMEM,
        out_shape=jax.ShapeDtypeStruct((frames, 4 * width), jnp.float32),
        scratch_shapes=[pltpu.VMEM((4 * width, size), jnp.float32)],
        name="whole",
    )(*(in_vmem(x) for x in pieces))


def in_vmem(x):
    return pltpu.with_memory_space_constraint(x, pltpu.VMEM)


def exchanged(pieces, axis):
    return lax.all_to_all(pieces, axis, 0, 0, tiled=True)


def to_everyone(shard, peers):
    return jnp.broadcast_to(shard[None], (peers, *shard.shape))


def swapped(x, core, across):
    cores, chips = lax.axis_size("core"), lax.axis_size("x")
    pairs = []
    for c in range(cores):
        for i in range(chips):
            to = (c ^ core) * chips + (i ^ across)
            pairs.append((c * chips + i, to))
    return lax.ppermute(x, ("core", "x"), pairs)


def all_summed(keep, give, dtype, scale, held=None):
    chip = keep + swapped(give, 1, 0)
    pieces = exchanged(to_everyone(chip, lax.axis_size("z")), "z")
    total = (jnp.sum(pieces, axis=0) * scale).astype(dtype)
    if held is not None:
        total, held = lax.optimization_barrier((total, held))
    return (total, swapped(total, 1, 0), swapped(total, 0, 1), swapped(total, 1, 1)), held


def local(data, shared_start):
    frames = data.shape[1]
    features = shared_start.shape[0]
    peers = lax.axis_size(("y", "x"))
    subjects = data.shape[0] * lax.axis_size(("z", "core"))
    size = padded(frames)
    packed, shared = packed_grams(data, shared_start.T, size)
    share = jnp.sum(exchanged(packed.reshape(peers, size // peers, size), ("y", "x")), axis=0)
    packed = exchanged(to_everyone(share, peers), ("y", "x")).reshape(size, size)
    keep, give = refits(packed, (shared,), frames, features, False)
    pieces, _ = all_summed(keep, give, jnp.bfloat16, 1.0 / subjects)
    keep, give, projections = refits(packed, pieces, frames, features, True)
    pieces, projections = all_summed(keep, give, jnp.float32, 1.0 / subjects, projections)
    response = whole(pieces, frames)
    return (projections[:, :, :frames], response.T)


def solution(mesh):
    sizes = dict(mesh.shape)
    cores, across = 2, 4
    shape = (sizes["subj"] // cores, cores, sizes["vox"] // across, across)
    chips = Mesh(mesh.devices.reshape(shape), ("z", "core", "y", "x"))
    placed = (P(("z", "core"), None, ("y", "x")), P())
    return jax.shard_map(
        local,
        mesh=chips,
        in_specs=placed,
        out_specs=(P(("z", "core"), None, None), P()),
        check_vma=False,
    )
```

```python
import functools

import jax
import jax.numpy as jnp
from jax import lax
from jax.experimental import pallas as pl
from jax.experimental.pallas import tpu as pltpu
from jax.sharding import Mesh, PartitionSpec as P

ITERS = 3
LANES = 128
VMEM = pl.BlockSpec(memory_space=pltpu.VMEM)


def padded(frames):
    return -(-frames // (2 * LANES)) * 2 * LANES


def positions(size):
    rows = lax.broadcasted_iota(jnp.int32, (size, size), 0)
    cols = lax.broadcasted_iota(jnp.int32, (size, size), 1)
    return rows, cols


def gram_kernel(data_ref, start_ref, packed_ref, shared_ref, sums_ref):
    step = pl.program_id(0)
    frames = data_ref.shape[1]

    @pl.when(step == 0)
    def _():
        sums_ref[...] = jnp.zeros_like(sums_ref)
        shared_ref[...] = jnp.zeros_like(shared_ref)
        shared_ref[:, 0:frames] = start_ref[...].T

    for subject in range(2):
        block = data_ref[subject]
        sums_ref[subject] += lax.dot_general(
            block, block, (((1,), (1,)), ((), ())), preferred_element_type=jnp.float32
        )

    @pl.when(step == pl.num_programs(0) - 1)
    def _():
        rows, cols = positions(frames)
        first, second = sums_ref[0], sums_ref[1]
        mixed = jnp.where(rows >= cols, first, second)
        diagonal = jnp.sum(jnp.where(rows == cols, second, 0.0), axis=1, keepdims=True)
        packed_ref[...] = jnp.zeros_like(packed_ref)
        packed_ref[0:frames, 0:frames] = mixed
        packed_ref[0:frames, frames : frames + 1] = diagonal


def packed_grams(data, start, size):
    subjects, frames, voxels = data.shape
    features = start.shape[1]
    tile = 2048
    return pl.pallas_call(
        gram_kernel,
        grid=(voxels // tile,),
        in_specs=[pl.BlockSpec((subjects, frames, tile), lambda i: (0, 0, i)), VMEM],
        out_specs=[VMEM, VMEM],
        out_shape=[
            pltpu.VMEM((size, size), jnp.float32),
            pltpu.VMEM((features, size), jnp.bfloat16),
        ],
        scratch_shapes=[pltpu.VMEM((subjects, frames, frames), jnp.float32)],
        name="grams",
    )(data, start)


def parts_of(x, count):
    parts = []
    for part in range(count):
        parts.append(x.astype(jnp.bfloat16))
        if part < count - 1:
            x = x - parts[-1].astype(jnp.float32)
    return parts


def product(a, b, dims=((1,), (0,))):
    return lax.dot_general(a, b, (dims, ((), ())), preferred_element_type=jnp.float32)


def halves(matrices):
    return [parts_of(matrix, 2) for matrix in matrices]


def times(a, b):
    high, low = b
    wide = jnp.concatenate([high, low], axis=1)
    out = product(jnp.concatenate(a, axis=1), jnp.concatenate([wide, wide], axis=0))
    return out[:, : high.shape[1]] + out[:, high.shape[1] :]


def unpacked(packed, frames):
    rows, cols = positions(packed.shape[0])
    diagonal = packed[:, frames : frames + 1]
    packed = jnp.where(cols < frames, packed, 0.0)
    flipped = packed.T
    return (
        jnp.where(rows >= cols, packed, flipped),
        jnp.where(rows == cols, diagonal, jnp.where(rows < cols, packed, flipped)),
    )


def refit(grams, shared):
    crossed = [sum(product(shared, part) for part in parts) for parts in grams]
    wide = shared.astype(jnp.float32)
    squares = [jnp.sum(cross * wide) + 1e-06 for cross in crossed]
    split = halves(crossed)
    both = [product(shared, jnp.concatenate(parts, axis=0), ((1,), (1,))) for parts in split]
    features = shared.shape[0]
    current = [
        (pair[:, :features] + pair[:, features:]) * (1.0 / square)
        for pair, square in zip(both, squares)
    ]
    taken, gain = None, 1.0
    for step in range(ITERS - 1):
        parts = halves(current)
        squared = [times(part, part) for part in parts]
        if step > 0:
            moved = [times(own, part) for own, part in zip(halves(taken), parts)]
        half = [1.5 * x - 0.5 * y for x, y in zip(current, squared)]
        cubed = [times(own, part) for own, part in zip(halves(half), parts)]
        if step > 0:
            taken = [1.5 * d + 0.5 * gain * x - 0.5 * y for d, x, y in zip(taken, current, moved)]
        else:
            taken = [0.5 * gain * x for x in current]
        gain *= 1.5
        current = [1.5 * x - 0.5 * y for x, y in zip(half, cubed)]
    moved = [against(own, part) for own, part in zip(halves(taken), split)]
    before = [gain * cross - part for cross, part in zip(crossed, moved)]
    return before, current, [1.0 / jnp.sqrt(square) for square in squares]


def against(a, b):
    high, low = b
    stacked = jnp.concatenate([high, high], axis=0)
    return product(jnp.concatenate(a, axis=1), stacked) + product(a[0], low)


def shares(keep_ref, give_ref, before_ref, current_ref, before, scales):
    width = keep_ref.shape[0]
    ahead, factor = [], []
    for piece in range(2):
        place = block(piece, width)
        ahead.append(sum(1.5 * scale * before_ref[s, place, :] for s, scale in enumerate(scales)))
        factor.append(
            jnp.concatenate(
                [0.5 * scale * current_ref[s, place, :] for s, scale in enumerate(scales)], axis=1
            )
        )
    high, low = parts_of(jnp.concatenate(factor, axis=0), 2)
    split = halves(before)
    upper = jnp.concatenate([parts[0] for parts in split], axis=0)
    lower = jnp.concatenate([parts[1] for parts in split], axis=0)
    moved = product(high, upper) + product(high, lower) + product(low, upper)
    keep_ref[...] = ahead[0] - moved[:width]
    give_ref[...] = ahead[1] - moved[width:]


def finish(grams, shared, keep_ref, give_ref, before_ref, current_ref):
    before, current, scales = refit(grams, shared)
    for subject in range(2):
        before_ref[subject] = before[subject]
        current_ref[subject] = current[subject]
    shares(keep_ref, give_ref, before_ref, current_ref, before, scales)
    return scales


def refit_kernel(frames, packed_ref, shared_ref, *refs):
    grams = [parts_of(gram, 3) for gram in unpacked(packed_ref[...], frames)]
    finish(grams, shared_ref[...], *refs)


def unpack_kernel(frames, packed_ref, parts_ref):
    for subject, gram in enumerate(unpacked(packed_ref[...], frames)):
        for part, half in enumerate(parts_of(gram, 2)):
            parts_ref[subject, part] = half


def last_kernel(parts_ref, own_ref, near_ref, far_ref, both_ref, *refs):
    *refs, scales_ref, shared_ref = refs
    for piece, piece_ref in enumerate((own_ref, near_ref, far_ref, both_ref)):
        shared_ref[block(piece, piece_ref.shape[0]), :] = piece_ref[...]
    grams = [[parts_ref[subject, part] for part in range(2)] for subject in range(2)]
    scales = finish(grams, shared_ref[...], *refs)
    for subject in range(2):
        scales_ref[subject] = jnp.full(scales_ref.shape[1:], scales[subject], jnp.float32)


def project_kernel(before_ref, current_ref, scales_ref, out_ref):
    for subject in range(2):
        before = before_ref[subject]
        moved = against(parts_of(current_ref[subject], 2), parts_of(before, 2))
        projected = (1.5 * before - 0.5 * moved) * scales_ref[subject, 0:1, 0:1]
        out_ref[subject] = projected.T[0 : out_ref.shape[1], :]


def block(piece, width):
    core, side = lax.axis_index("core"), lax.axis_index("x") % 2
    core = 1 - core if piece % 2 else core
    side = 1 - side if piece // 2 else side
    return pl.ds(pl.multiple_of((2 * side + core) * width, width), width)


def call(kernel, name, out, args, scratch=()):
    return pl.pallas_call(
        kernel,
        in_specs=[VMEM] * len(args),
        out_specs=[VMEM] * len(out),
        out_shape=out,
        scratch_shapes=scratch,
        name=name,
    )(*(in_vmem(x) for x in args))


def whole_kernel(*refs):
    pieces, out_ref, whole_ref = refs[:4], refs[4], refs[5]
    for piece, piece_ref in enumerate(pieces):
        whole_ref[block(piece, piece_ref.shape[0]), :] = piece_ref[...]
    out_ref[...] = whole_ref[...].T[0 : out_ref.shape[0], :]


def in_vmem(x):
    return pltpu.with_memory_space_constraint(x, pltpu.VMEM)


def exchanged(pieces, axis):
    return lax.all_to_all(pieces, axis, 0, 0, tiled=True)


def to_everyone(shard, peers):
    return jnp.broadcast_to(shard[None], (peers, *shard.shape))


def swapped(x, core, across):
    cores, chips = lax.axis_size("core"), lax.axis_size("x")
    pairs = []
    for c in range(cores):
        for i in range(chips):
            to = (c ^ core) * chips + (i ^ across)
            pairs.append((c * chips + i, to))
    return lax.ppermute(x, ("core", "x"), pairs)


def all_summed(keep, give, dtype, scale, held):
    chip = keep + swapped(give, 1, 0)
    pieces = exchanged(to_everyone(chip, lax.axis_size("z")), "z")
    total = (jnp.sum(pieces, axis=0) * scale).astype(dtype)
    total, held = lax.optimization_barrier((total, held))
    return (total, swapped(total, 1, 0), swapped(total, 0, 1), swapped(total, 1, 1)), held


def local(data, shared_start):
    frames = data.shape[1]
    features = shared_start.shape[0]
    peers = lax.axis_size(("y", "x"))
    subjects = data.shape[0] * lax.axis_size(("z", "core"))
    size = padded(frames)
    packed, shared = packed_grams(data, shared_start.T, size)
    share = jnp.sum(exchanged(packed.reshape(peers, size // peers, size), ("y", "x")), axis=0)
    packed = exchanged(to_everyone(share, peers), ("y", "x")).reshape(size, size)
    blocks = [pltpu.VMEM((features // 4, size), jnp.float32)] * 2
    crosses = pltpu.VMEM((2, features, size), jnp.float32)
    squares = pltpu.VMEM((2, features, features), jnp.float32)
    keep, give = call(
        functools.partial(refit_kernel, frames), "refits", blocks, (packed, shared),
        [crosses, squares],
    )
    pieces, packed = all_summed(keep, give, jnp.bfloat16, 1.0 / subjects, packed)
    (parts,) = call(
        functools.partial(unpack_kernel, frames), "unpack",
        [pltpu.VMEM((2, 2, size, size), jnp.bfloat16)], (packed,),
    )
    keep, give, *state = call(
        last_kernel, "refits_last",
        [*blocks, crosses, squares, pltpu.VMEM((2, 8, LANES), jnp.float32)],
        (parts, *pieces), [pltpu.VMEM((features, size), jnp.bfloat16)],
    )
    pieces, state = all_summed(keep, give, jnp.float32, 1.0 / subjects, state)
    (projections,) = call(
        project_kernel, "project",
        [jax.ShapeDtypeStruct((2, frames, features), jnp.float32)], state,
    )
    (response,) = call(
        whole_kernel, "whole", [jax.ShapeDtypeStruct((frames, features), jnp.float32)], pieces,
        [pltpu.VMEM((features, size), jnp.float32)],
    )
    return (jnp.swapaxes(projections, 1, 2), response.T)


def solution(mesh):
    sizes = dict(mesh.shape)
    cores, across = 2, 4
    shape = (sizes["subj"] // cores, cores, sizes["vox"] // across, across)
    chips = Mesh(mesh.devices.reshape(shape), ("z", "core", "y", "x"))
    placed = (P(("z", "core"), None, ("y", "x")), P())
    return jax.shard_map(
        local,
        mesh=chips,
        in_specs=placed,
        out_specs=(P(("z", "core"), None, None), P()),
        check_vma=False,
    )
```

```python
import functools

import jax
import jax.numpy as jnp
from jax import lax
from jax.experimental import pallas as pl
from jax.experimental.pallas import tpu as pltpu
from jax.sharding import Mesh, PartitionSpec as P

ITERS = 3
LANES = 128
VMEM = pl.BlockSpec(memory_space=pltpu.VMEM)


def padded(frames):
    return -(-frames // (2 * LANES)) * 2 * LANES


def positions(size):
    rows = lax.broadcasted_iota(jnp.int32, (size, size), 0)
    cols = lax.broadcasted_iota(jnp.int32, (size, size), 1)
    return rows, cols


def gram_kernel(data_ref, start_ref, packed_ref, shared_ref, sums_ref):
    frames = data_ref.shape[1]

    @pl.when(pl.program_id(0) == 0)
    def _():
        shared_ref[...] = jnp.zeros_like(shared_ref)
        shared_ref[:, 0:frames] = start_ref[...].T
        packed_ref[...] = jnp.zeros_like(packed_ref)
        for subject in range(2):
            block = data_ref[subject]
            sums_ref[subject] = product(block, block, ((1,), (1,)))

    @pl.when(pl.program_id(0) == 1)
    def _():
        first, second = (
            sums_ref[subject] + product(data_ref[subject], data_ref[subject], ((1,), (1,)))
            for subject in range(2)
        )
        rows, cols = positions(frames)
        packed_ref[0:frames, 0:frames] = jnp.where(rows >= cols, first, second)
        packed_ref[0:frames, frames : frames + 1] = jnp.sum(
            jnp.where(rows == cols, second, 0.0), axis=1, keepdims=True
        )


def packed_grams(data, start, size):
    subjects, frames, voxels = data.shape
    features = start.shape[1]
    return pl.pallas_call(
        gram_kernel,
        grid=(2,),
        in_specs=[pl.BlockSpec((subjects, frames, voxels // 2), lambda i: (0, 0, i)), VMEM],
        out_specs=[VMEM, VMEM],
        out_shape=[
            pltpu.VMEM((size, size), jnp.float32),
            pltpu.VMEM((features, size), jnp.bfloat16),
        ],
        scratch_shapes=[pltpu.VMEM((subjects, frames, frames), jnp.float32)],
        name="grams",
    )(data, start)


def parts_of(x, count):
    parts = []
    for part in range(count):
        parts.append(x.astype(jnp.bfloat16))
        if part < count - 1:
            x = x - parts[-1].astype(jnp.float32)
    return parts


def product(a, b, dims=((1,), (0,))):
    return lax.dot_general(a, b, (dims, ((), ())), preferred_element_type=jnp.float32)


def halves(matrices):
    return [parts_of(matrix, 2) for matrix in matrices]


def times(a, b):
    high, low = b
    wide = jnp.concatenate([high, low], axis=1)
    out = product(jnp.concatenate(a, axis=1), jnp.concatenate([wide, wide], axis=0))
    return out[:, : high.shape[1]] + out[:, high.shape[1] :]


def unpacked(packed, frames):
    rows, cols = positions(packed.shape[0])
    diagonal = packed[:, frames : frames + 1]
    packed = jnp.where(cols < frames, packed, 0.0)
    flipped = packed.T
    return (
        jnp.where(rows >= cols, packed, flipped),
        jnp.where(rows == cols, diagonal, jnp.where(rows < cols, packed, flipped)),
    )


def refit(grams, shared, exact):
    crossed = [sum(product(shared, part) for part in parts) for parts in grams]
    wide = shared.astype(jnp.float32)
    squares = [jnp.sum(cross * wide) + 1e-06 for cross in crossed]
    split = [parts_of(cross, 3 if exact else 2) for cross in crossed]
    both = [product(shared, jnp.concatenate(parts[:2], axis=0), ((1,), (1,))) for parts in split]
    features = shared.shape[0]
    firsts = [pair[:, :features] + pair[:, features:] for pair in both]
    if exact:
        lows = [product(shared, parts[2], ((1,), (1,))) for parts in split]
        firsts = [first + low for first, low in zip(firsts, lows)]
    current = [first * (1.0 / square) for first, square in zip(firsts, squares)]
    taken, gain = None, 1.0
    for step in range(ITERS - 1):
        parts = halves(current)
        squared = [times(part, part) for part in parts]
        if step > 0:
            moved = [times(own, part) for own, part in zip(halves(taken), parts)]
        half = [1.5 * x - 0.5 * y for x, y in zip(current, squared)]
        cubed = [times(own, part) for own, part in zip(halves(half), parts)]
        if step > 0:
            taken = [1.5 * d + 0.5 * gain * x - 0.5 * y for d, x, y in zip(taken, current, moved)]
        else:
            taken = [0.5 * gain * x for x in current]
        gain *= 1.5
        current = [1.5 * x - 0.5 * y for x, y in zip(half, cubed)]
    moved = [against(own, part) for own, part in zip(halves(taken), split)]
    before = [gain * cross - part for cross, part in zip(crossed, moved)]
    return before, current, [1.0 / jnp.sqrt(square) for square in squares]


def against(a, b):
    high, low = b[:2]
    stacked = jnp.concatenate([high, high], axis=0)
    return product(jnp.concatenate(a, axis=1), stacked) + product(a[0], low)


def shares(keep_ref, give_ref, before_ref, current_ref, before, scales):
    width = keep_ref.shape[0]
    ahead, factor = [], []
    for piece in range(2):
        place = block(piece, width)
        ahead.append(sum(1.5 * scale * before_ref[s, place, :] for s, scale in enumerate(scales)))
        factor.append(
            jnp.concatenate(
                [0.5 * scale * current_ref[s, place, :] for s, scale in enumerate(scales)], axis=1
            )
        )
    high, low = parts_of(jnp.concatenate(factor, axis=0), 2)
    split = halves(before)
    upper = jnp.concatenate([parts[0] for parts in split], axis=0)
    lower = jnp.concatenate([parts[1] for parts in split], axis=0)
    moved = product(high, upper) + product(high, lower) + product(low, upper)
    keep_ref[...] = ahead[0] - moved[:width]
    give_ref[...] = ahead[1] - moved[width:]


def finish(grams, shared, exact, keep_ref, give_ref, before_ref, current_ref):
    before, current, scales = refit(grams, shared, exact)
    for subject in range(2):
        before_ref[subject] = before[subject]
        current_ref[subject] = current[subject]
    shares(keep_ref, give_ref, before_ref, current_ref, before, scales)
    return scales


def refit_kernel(frames, packed_ref, shared_ref, *refs):
    grams = [parts_of(gram, 3) for gram in unpacked(packed_ref[...], frames)]
    finish(grams, shared_ref[...], True, *refs)


def unpack_kernel(frames, packed_ref, parts_ref):
    for subject, gram in enumerate(unpacked(packed_ref[...], frames)):
        for part, half in enumerate(parts_of(gram, 3)):
            parts_ref[subject, part] = half


def last_kernel(parts_ref, own_ref, both_ref, near_ref, far_ref, *refs):
    *refs, scales_ref, shared_ref = refs
    for piece, piece_ref in enumerate((own_ref, near_ref, far_ref, both_ref)):
        shared_ref[block(piece, piece_ref.shape[0]), :] = piece_ref[...]
    grams = [[parts_ref[subject, part] for part in range(3)] for subject in range(2)]
    scales = finish(grams, shared_ref[...], False, *refs)
    for subject in range(2):
        scales_ref[subject] = jnp.full(scales_ref.shape[1:], scales[subject], jnp.float32)


def project_kernel(before_ref, current_ref, scales_ref, out_ref):
    for subject in range(2):
        before = before_ref[subject]
        moved = against(parts_of(current_ref[subject], 2), parts_of(before, 2))
        projected = (1.5 * before - 0.5 * moved) * scales_ref[subject, 0:1, 0:1]
        out_ref[subject] = projected.T[0 : out_ref.shape[1], :]


def block(piece, width):
    core, side = lax.axis_index("core"), lax.axis_index("x") % 2
    core = 1 - core if piece % 2 else core
    side = 1 - side if piece // 2 else side
    return pl.ds(pl.multiple_of((2 * side + core) * width, width), width)


def call(kernel, name, out, args, scratch=()):
    return pl.pallas_call(
        kernel,
        in_specs=[VMEM] * len(args),
        out_specs=[VMEM] * len(out),
        out_shape=out,
        scratch_shapes=scratch,
        name=name,
    )(*(in_vmem(x) for x in args))


def whole_kernel(own_ref, both_ref, near_ref, far_ref, out_ref, whole_ref):
    for piece, piece_ref in enumerate((own_ref, near_ref, far_ref, both_ref)):
        whole_ref[block(piece, piece_ref.shape[0]), :] = piece_ref[...]
    out_ref[...] = whole_ref[...].T[0 : out_ref.shape[0], :]


def in_vmem(x):
    return pltpu.with_memory_space_constraint(x, pltpu.VMEM)


def exchanged(pieces, axis):
    return lax.all_to_all(pieces, axis, 0, 0, tiled=True)


def to_everyone(shard, peers):
    return jnp.broadcast_to(shard[None], (peers, *shard.shape))


def swapped(x, core, across):
    cores, chips = lax.axis_size("core"), lax.axis_size("x")
    pairs = []
    for c in range(cores):
        for i in range(chips):
            to = (c ^ core) * chips + (i ^ across)
            pairs.append((c * chips + i, to))
    return lax.ppermute(x, ("core", "x"), pairs)


def all_summed(keep, give, dtype, scale, held):
    chip = keep + swapped(give, 1, 0)
    pieces = exchanged(to_everyone(chip, lax.axis_size("z")), "z")
    total = (jnp.sum(pieces, axis=0) * scale).astype(dtype)
    total, held = lax.optimization_barrier((total, held))
    return (total, swapped(total, 1, 1), swapped(total, 1, 0), swapped(total, 0, 1)), held


def local(data, shared_start):
    frames = data.shape[1]
    features = shared_start.shape[0]
    peers = lax.axis_size(("y", "x"))
    subjects = data.shape[0] * lax.axis_size(("z", "core"))
    size = padded(frames)
    packed, shared = packed_grams(data, shared_start.T, size)
    share = jnp.sum(exchanged(packed.reshape(peers, size // peers, size), ("y", "x")), axis=0)
    packed = exchanged(to_everyone(share, peers), ("y", "x")).reshape(size, size)
    blocks = [pltpu.VMEM((features // 4, size), jnp.float32)] * 2
    crosses = pltpu.VMEM((2, features, size), jnp.float32)
    squares = pltpu.VMEM((2, features, features), jnp.float32)
    keep, give = call(
        functools.partial(refit_kernel, frames), "refits", blocks, (packed, shared),
        [crosses, squares],
    )
    pieces, packed = all_summed(keep, give, jnp.bfloat16, 1.0 / subjects, packed)
    (parts,) = call(
        functools.partial(unpack_kernel, frames), "unpack",
        [pltpu.VMEM((2, 3, size, size), jnp.bfloat16)], (packed,),
    )
    keep, give, *state = call(
        last_kernel, "refits_last",
        [*blocks, crosses, squares, pltpu.VMEM((2, 8, LANES), jnp.float32)],
        (parts, *pieces), [pltpu.VMEM((features, size), jnp.bfloat16)],
    )
    pieces, state = all_summed(keep, give, jnp.float32, 1.0 / subjects, state)
    (projections,) = call(
        project_kernel, "project",
        [jax.ShapeDtypeStruct((2, frames, features), jnp.float32)], state,
    )
    (response,) = call(
        whole_kernel, "whole", [jax.ShapeDtypeStruct((frames, features), jnp.float32)], pieces,
        [pltpu.VMEM((features, size), jnp.float32)],
    )
    return (jnp.swapaxes(projections, 1, 2), response.T)


def solution(mesh):
    sizes = dict(mesh.shape)
    cores, across = 2, 4
    shape = (sizes["subj"] // cores, cores, sizes["vox"] // across, across)
    chips = Mesh(mesh.devices.reshape(shape), ("z", "core", "y", "x"))
    placed = (P(("z", "core"), None, ("y", "x")), P())
    return jax.shard_map(
        local,
        mesh=chips,
        in_specs=placed,
        out_specs=(P(("z", "core"), None, None), P()),
        check_vma=False,
    )
```

```python
import functools

import jax
import jax.numpy as jnp
from jax import lax
from jax.experimental import pallas as pl
from jax.experimental.pallas import tpu as pltpu
from jax.sharding import Mesh, PartitionSpec as P

ITERS = 3
LANES = 128
VMEM = pl.BlockSpec(memory_space=pltpu.VMEM)


def padded(frames):
    return -(-frames // (2 * LANES)) * 2 * LANES


def positions(size):
    rows = lax.broadcasted_iota(jnp.int32, (size, size), 0)
    cols = lax.broadcasted_iota(jnp.int32, (size, size), 1)
    return rows, cols


def gram_kernel(data_ref, start_ref, packed_ref, shared_ref, sums_ref):
    frames = data_ref.shape[1]

    @pl.when(pl.program_id(0) == 0)
    def _():
        shared_ref[...] = jnp.zeros_like(shared_ref)
        shared_ref[:, 0:frames] = start_ref[...].T
        packed_ref[...] = jnp.zeros_like(packed_ref)
        for subject in range(2):
            block = data_ref[subject]
            sums_ref[subject] = product(block, block, ((1,), (1,)))

    @pl.when(pl.program_id(0) == 1)
    def _():
        first, second = (
            sums_ref[subject] + product(data_ref[subject], data_ref[subject], ((1,), (1,)))
            for subject in range(2)
        )
        rows, cols = positions(frames)
        packed_ref[0:frames, 0:frames] = jnp.where(rows >= cols, first, second)
        packed_ref[0:frames, frames : frames + 1] = jnp.sum(
            jnp.where(rows == cols, second, 0.0), axis=1, keepdims=True
        )


def packed_grams(data, start, size):
    subjects, frames, voxels = data.shape
    features = start.shape[1]
    return pl.pallas_call(
        gram_kernel,
        grid=(2,),
        in_specs=[pl.BlockSpec((subjects, frames, voxels // 2), lambda i: (0, 0, i)), VMEM],
        out_specs=[VMEM, VMEM],
        out_shape=[
            pltpu.VMEM((size, size), jnp.float32),
            pltpu.VMEM((features, size), jnp.bfloat16),
        ],
        scratch_shapes=[pltpu.VMEM((subjects, frames, frames), jnp.float32)],
        name="grams",
    )(data, start)


def parts_of(x, count):
    parts = []
    for part in range(count):
        parts.append(x.astype(jnp.bfloat16))
        if part < count - 1:
            x = x - parts[-1].astype(jnp.float32)
    return parts


def product(a, b, dims=((1,), (0,))):
    return lax.dot_general(a, b, (dims, ((), ())), preferred_element_type=jnp.float32)


def halves(matrices):
    return [parts_of(matrix, 2) for matrix in matrices]


def times(a, b):
    high, low = b
    wide = jnp.concatenate([high, low], axis=1)
    out = product(jnp.concatenate(a, axis=1), jnp.concatenate([wide, wide], axis=0))
    return out[:, : high.shape[1]] + out[:, high.shape[1] :]


def unpacked(packed, frames):
    rows, cols = positions(packed.shape[0])
    diagonal = packed[:, frames : frames + 1]
    packed = jnp.where(cols < frames, packed, 0.0)
    flipped = packed.T
    return (
        jnp.where(rows >= cols, packed, flipped),
        jnp.where(rows == cols, diagonal, jnp.where(rows < cols, packed, flipped)),
    )


def refit(grams, shared, exact):
    crossed = [sum(product(shared, part) for part in parts) for parts in grams]
    wide = shared.astype(jnp.float32)
    squares = [jnp.sum(cross * wide) + 1e-06 for cross in crossed]
    split = [parts_of(cross, 3 if exact else 2) for cross in crossed]
    both = [product(shared, jnp.concatenate(parts[:2], axis=0), ((1,), (1,))) for parts in split]
    features = shared.shape[0]
    firsts = [pair[:, :features] + pair[:, features:] for pair in both]
    if exact:
        lows = [product(shared, parts[2], ((1,), (1,))) for parts in split]
        firsts = [first + low for first, low in zip(firsts, lows)]
    current = [first * (1.0 / square) for first, square in zip(firsts, squares)]
    taken, gain = None, 1.0
    for step in range(ITERS - 1):
        parts = halves(current)
        squared = [times(part, part) for part in parts]
        if step > 0:
            moved = [times(own, part) for own, part in zip(halves(taken), parts)]
        half = [1.5 * x - 0.5 * y for x, y in zip(current, squared)]
        cubed = [times(own, part) for own, part in zip(halves(half), parts)]
        if step > 0:
            taken = [1.5 * d + 0.5 * gain * x - 0.5 * y for d, x, y in zip(taken, current, moved)]
        else:
            taken = [0.5 * gain * x for x in current]
        gain *= 1.5
        current = [1.5 * x - 0.5 * y for x, y in zip(half, cubed)]
    moved = [against(own, part) for own, part in zip(halves(taken), split)]
    before = [gain * cross - part for cross, part in zip(crossed, moved)]
    return before, current, [1.0 / jnp.sqrt(square) for square in squares]


def against(a, b):
    high, low = b[:2]
    stacked = jnp.concatenate([high, high], axis=0)
    return product(jnp.concatenate(a, axis=1), stacked) + product(a[0], low)


def shares(keep_ref, give_ref, before_ref, current_ref, before, scales):
    width = keep_ref.shape[0]
    ahead, factor = [], []
    for piece in range(2):
        place = block(piece, width)
        ahead.append(sum(1.5 * scale * before_ref[s, place, :] for s, scale in enumerate(scales)))
        factor.append(
            jnp.concatenate(
                [0.5 * scale * current_ref[s, place, :] for s, scale in enumerate(scales)], axis=1
            )
        )
    high, low = parts_of(jnp.concatenate(factor, axis=0), 2)
    split = halves(before)
    upper = jnp.concatenate([parts[0] for parts in split], axis=0)
    lower = jnp.concatenate([parts[1] for parts in split], axis=0)
    moved = product(high, upper) + product(high, lower) + product(low, upper)
    keep_ref[...] = ahead[0] - moved[:width]
    give_ref[...] = ahead[1] - moved[width:]


def finish(grams, shared, exact, keep_ref, give_ref, before_ref, current_ref):
    before, current, scales = refit(grams, shared, exact)
    for subject in range(2):
        before_ref[subject] = before[subject]
        current_ref[subject] = current[subject]
    shares(keep_ref, give_ref, before_ref, current_ref, before, scales)
    return scales


def refit_kernel(frames, packed_ref, shared_ref, *refs):
    grams = [parts_of(gram, 3) for gram in unpacked(packed_ref[...], frames)]
    finish(grams, shared_ref[...], True, *refs)


def unpack_kernel(frames, packed_ref, parts_ref):
    for subject, gram in enumerate(unpacked(packed_ref[...], frames)):
        for part, half in enumerate(parts_of(gram, 3)):
            parts_ref[subject, part] = half


def last_kernel(parts_ref, own_ref, near_ref, far_ref, both_ref, *refs):
    *refs, scales_ref, shared_ref = refs
    for piece, piece_ref in enumerate((own_ref, near_ref, far_ref, both_ref)):
        shared_ref[block(piece, piece_ref.shape[0]), :] = piece_ref[...]
    grams = [[parts_ref[subject, part] for part in range(3)] for subject in range(2)]
    scales = finish(grams, shared_ref[...], False, *refs)
    for subject in range(2):
        scales_ref[subject] = jnp.full(scales_ref.shape[1:], scales[subject], jnp.float32)


def project_kernel(before_ref, current_ref, scales_ref, out_ref):
    for subject in range(2):
        before = before_ref[subject]
        moved = against(parts_of(current_ref[subject], 2), parts_of(before, 2))
        projected = (1.5 * before - 0.5 * moved) * scales_ref[subject, 0:1, 0:1]
        out_ref[subject] = projected.T[0 : out_ref.shape[1], :]


def block(piece, width):
    core, side = lax.axis_index("core"), lax.axis_index("x") % 2
    core = 1 - core if piece % 2 else core
    side = 1 - side if piece // 2 else side
    return pl.ds(pl.multiple_of((2 * side + core) * width, width), width)


def call(kernel, name, out, args, scratch=()):
    return pl.pallas_call(
        kernel,
        in_specs=[VMEM] * len(args),
        out_specs=[VMEM] * len(out),
        out_shape=out,
        scratch_shapes=scratch,
        name=name,
    )(*(in_vmem(x) for x in args))


def whole_kernel(own_ref, near_ref, far_ref, both_ref, out_ref, whole_ref):
    for piece, piece_ref in enumerate((own_ref, near_ref, far_ref, both_ref)):
        whole_ref[block(piece, piece_ref.shape[0]), :] = piece_ref[...]
    out_ref[...] = whole_ref[...].T[0 : out_ref.shape[0], :]


def in_vmem(x):
    return pltpu.with_memory_space_constraint(x, pltpu.VMEM)


def exchanged(pieces, axis):
    return lax.all_to_all(pieces, axis, 0, 0, tiled=True)


def to_everyone(shard, peers):
    return jnp.broadcast_to(shard[None], (peers, *shard.shape))


def swapped(x, core, across):
    cores, chips = lax.axis_size("core"), lax.axis_size("x")
    pairs = []
    for c in range(cores):
        for i in range(chips):
            to = (c ^ core) * chips + (i ^ across)
            pairs.append((c * chips + i, to))
    return lax.ppermute(x, ("core", "x"), pairs)


def along(x, mask):
    chips = lax.axis_size("z")
    return lax.ppermute(x, "z", [(chip, chip ^ mask) for chip in range(chips)])


def four_kernel(own_ref, near_ref, far_ref, next_ref, out_ref):
    out_ref[...] = (own_ref[...] + near_ref[...]) + (far_ref[...] + next_ref[...])


def all_summed(keep, give, dtype, scale, held):
    total = keep + swapped(give, 1, 0)
    (total,) = call(
        four_kernel, "four", [pltpu.VMEM(keep.shape, jnp.float32)],
        (total, along(total, 1), along(total, 6), along(total, 7)),
    )
    total = ((total + along(total, 2)) * scale).astype(dtype)
    total, held = lax.optimization_barrier((total, held))
    return (total, swapped(total, 1, 0), swapped(total, 0, 1), swapped(total, 1, 1)), held


def local(data, shared_start):
    frames = data.shape[1]
    features = shared_start.shape[0]
    peers = lax.axis_size(("y", "x"))
    subjects = data.shape[0] * lax.axis_size(("z", "core"))
    size = padded(frames)
    packed, shared = packed_grams(data, shared_start.T, size)
    share = jnp.sum(exchanged(packed.reshape(peers, size // peers, size), ("y", "x")), axis=0)
    packed = exchanged(to_everyone(share, peers), ("y", "x")).reshape(size, size)
    blocks = [pltpu.VMEM((features // 4, size), jnp.float32)] * 2
    crosses = pltpu.VMEM((2, features, size), jnp.float32)
    squares = pltpu.VMEM((2, features, features), jnp.float32)
    keep, give = call(
        functools.partial(refit_kernel, frames), "refits", blocks, (packed, shared),
        [crosses, squares],
    )
    pieces, packed = all_summed(keep, give, jnp.bfloat16, 1.0 / subjects, packed)
    (parts,) = call(
        functools.partial(unpack_kernel, frames), "unpack",
        [pltpu.VMEM((2, 3, size, size), jnp.bfloat16)], (packed,),
    )
    keep, give, *state = call(
        last_kernel, "refits_last",
        [*blocks, crosses, squares, pltpu.VMEM((2, 8, LANES), jnp.float32)],
        (parts, *pieces), [pltpu.VMEM((features, size), jnp.bfloat16)],
    )
    pieces, state = all_summed(keep, give, jnp.float32, 1.0 / subjects, state)
    (projections,) = call(
        project_kernel, "project",
        [jax.ShapeDtypeStruct((2, frames, features), jnp.float32)], state,
    )
    (response,) = call(
        whole_kernel, "whole", [jax.ShapeDtypeStruct((frames, features), jnp.float32)], pieces,
        [pltpu.VMEM((features, size), jnp.float32)],
    )
    return (jnp.swapaxes(projections, 1, 2), response.T)


def solution(mesh):
    sizes = dict(mesh.shape)
    cores, across = 2, 4
    shape = (sizes["subj"] // cores, cores, sizes["vox"] // across, across)
    chips = Mesh(mesh.devices.reshape(shape), ("z", "core", "y", "x"))
    placed = (P(("z", "core"), None, ("y", "x")), P())
    return jax.shard_map(
        local,
        mesh=chips,
        in_specs=placed,
        out_specs=(P(("z", "core"), None, None), P()),
        check_vma=False,
    )
```

```python
import functools

import jax
import jax.numpy as jnp
from jax import lax
from jax.experimental import pallas as pl
from jax.experimental.pallas import tpu as pltpu
from jax.sharding import Mesh, PartitionSpec as P

ITERS = 3
LANES = 128
VMEM = pl.BlockSpec(memory_space=pltpu.VMEM)


def padded(frames):
    return -(-frames // (2 * LANES)) * 2 * LANES


def positions(size):
    rows = lax.broadcasted_iota(jnp.int32, (size, size), 0)
    cols = lax.broadcasted_iota(jnp.int32, (size, size), 1)
    return rows, cols


def gram_kernel(data_ref, start_ref, packed_ref, shared_ref, sums_ref):
    frames = data_ref.shape[1]

    @pl.when(pl.program_id(0) == 0)
    def _():
        shared_ref[...] = jnp.zeros_like(shared_ref)
        shared_ref[:, 0:frames] = start_ref[...].T
        packed_ref[...] = jnp.zeros_like(packed_ref)
        for subject in range(2):
            block = data_ref[subject]
            sums_ref[subject] = product(block, block, ((1,), (1,)))

    @pl.when(pl.program_id(0) == 1)
    def _():
        first, second = (
            sums_ref[subject] + product(data_ref[subject], data_ref[subject], ((1,), (1,)))
            for subject in range(2)
        )
        rows, cols = positions(frames)
        packed_ref[0:frames, 0:frames] = jnp.where(rows >= cols, first, second)
        packed_ref[0:frames, frames : frames + 1] = jnp.sum(
            jnp.where(rows == cols, second, 0.0), axis=1, keepdims=True
        )


def packed_grams(data, start, size):
    subjects, frames, voxels = data.shape
    features = start.shape[1]
    return pl.pallas_call(
        gram_kernel,
        grid=(2,),
        in_specs=[pl.BlockSpec((subjects, frames, voxels // 2), lambda i: (0, 0, i)), VMEM],
        out_specs=[VMEM, VMEM],
        out_shape=[
            pltpu.VMEM((size, size), jnp.float32),
            pltpu.VMEM((features, size), jnp.bfloat16),
        ],
        scratch_shapes=[pltpu.VMEM((subjects, frames, frames), jnp.float32)],
        name="grams",
    )(data, start)


def parts_of(x, count):
    parts = []
    for part in range(count):
        parts.append(x.astype(jnp.bfloat16))
        if part < count - 1:
            x = x - parts[-1].astype(jnp.float32)
    return parts


def product(a, b, dims=((1,), (0,))):
    return lax.dot_general(a, b, (dims, ((), ())), preferred_element_type=jnp.float32)


def halves(matrices):
    return [parts_of(matrix, 2) for matrix in matrices]


def times(a, b):
    high, low = b
    wide = jnp.concatenate([high, low], axis=1)
    out = product(jnp.concatenate(a, axis=1), jnp.concatenate([wide, wide], axis=0))
    return out[:, : high.shape[1]] + out[:, high.shape[1] :]


def unpacked(packed, frames):
    rows, cols = positions(packed.shape[0])
    diagonal = packed[:, frames : frames + 1]
    packed = jnp.where(cols < frames, packed, 0.0)
    flipped = packed.T
    return (
        jnp.where(rows >= cols, packed, flipped),
        jnp.where(rows == cols, diagonal, jnp.where(rows < cols, packed, flipped)),
    )


def refit(grams, shared, exact):
    crossed = [sum(product(shared, part) for part in parts) for parts in grams]
    wide = shared.astype(jnp.float32)
    squares = [jnp.sum(cross * wide) + 1e-06 for cross in crossed]
    split = [parts_of(cross, 3 if exact else 2) for cross in crossed]
    both = [product(shared, jnp.concatenate(parts[:2], axis=0), ((1,), (1,))) for parts in split]
    features = shared.shape[0]
    firsts = [pair[:, :features] + pair[:, features:] for pair in both]
    if exact:
        lows = [product(shared, parts[2], ((1,), (1,))) for parts in split]
        firsts = [first + low for first, low in zip(firsts, lows)]
    current = [first * (1.0 / square) for first, square in zip(firsts, squares)]
    taken, gain = None, 1.0
    for step in range(ITERS - 1):
        parts = halves(current)
        squared = [times(part, part) for part in parts]
        if step > 0:
            moved = [times(own, part) for own, part in zip(halves(taken), parts)]
        half = [1.5 * x - 0.5 * y for x, y in zip(current, squared)]
        cubed = [times(own, part) for own, part in zip(halves(half), parts)]
        if step > 0:
            taken = [1.5 * d + 0.5 * gain * x - 0.5 * y for d, x, y in zip(taken, current, moved)]
        else:
            taken = [0.5 * gain * x for x in current]
        gain *= 1.5
        current = [1.5 * x - 0.5 * y for x, y in zip(half, cubed)]
    moved = [against(own, part) for own, part in zip(halves(taken), split)]
    before = [gain * cross - part for cross, part in zip(crossed, moved)]
    return before, current, [1.0 / jnp.sqrt(square) for square in squares]


def against(a, b):
    high, low = b[:2]
    stacked = jnp.concatenate([high, high], axis=0)
    return product(jnp.concatenate(a, axis=1), stacked) + product(a[0], low)


def shares(keep_ref, give_ref, before_ref, current_ref, before, scales):
    width = keep_ref.shape[0]
    ahead, factor = [], []
    for piece in range(2):
        place = block(piece, width)
        ahead.append(sum(1.5 * scale * before_ref[s, place, :] for s, scale in enumerate(scales)))
        factor.append(
            jnp.concatenate(
                [0.5 * scale * current_ref[s, place, :] for s, scale in enumerate(scales)], axis=1
            )
        )
    high, low = parts_of(jnp.concatenate(factor, axis=0), 2)
    split = halves(before)
    upper = jnp.concatenate([parts[0] for parts in split], axis=0)
    lower = jnp.concatenate([parts[1] for parts in split], axis=0)
    moved = product(high, upper) + product(high, lower) + product(low, upper)
    keep_ref[...] = ahead[0] - moved[:width]
    give_ref[...] = ahead[1] - moved[width:]


def finish(grams, shared, exact, keep_ref, give_ref, before_ref, current_ref):
    before, current, scales = refit(grams, shared, exact)
    for subject in range(2):
        before_ref[subject] = before[subject]
        current_ref[subject] = current[subject]
    shares(keep_ref, give_ref, before_ref, current_ref, before, scales)
    return scales


def refit_kernel(frames, packed_ref, shared_ref, *refs):
    grams = [parts_of(gram, 3) for gram in unpacked(packed_ref[...], frames)]
    finish(grams, shared_ref[...], True, *refs)


def unpack_kernel(frames, packed_ref, parts_ref):
    for subject, gram in enumerate(unpacked(packed_ref[...], frames)):
        for part, half in enumerate(parts_of(gram, 3)):
            parts_ref[subject, part] = half


def last_kernel(parts_ref, own_ref, near_ref, far_ref, both_ref, *refs):
    *refs, scales_ref, shared_ref = refs
    for piece, piece_ref in enumerate((own_ref, near_ref, far_ref, both_ref)):
        shared_ref[block(piece, piece_ref.shape[0]), :] = piece_ref[...]
    grams = [[parts_ref[subject, part] for part in range(3)] for subject in range(2)]
    scales = finish(grams, shared_ref[...], False, *refs)
    for subject in range(2):
        scales_ref[subject] = jnp.full(scales_ref.shape[1:], scales[subject], jnp.float32)


def project_kernel(before_ref, current_ref, scales_ref, out_ref):
    for subject in range(2):
        before = before_ref[subject]
        moved = against(parts_of(current_ref[subject], 2), parts_of(before, 2))
        projected = (1.5 * before - 0.5 * moved) * scales_ref[subject, 0:1, 0:1]
        out_ref[subject] = projected.T[0 : out_ref.shape[1], :]


def block(piece, width):
    core, side = lax.axis_index("core"), lax.axis_index("x") % 2
    core = 1 - core if piece % 2 else core
    side = 1 - side if piece // 2 else side
    return pl.ds(pl.multiple_of((2 * side + core) * width, width), width)


def call(kernel, name, out, args, scratch=()):
    return pl.pallas_call(
        kernel,
        in_specs=[VMEM] * len(args),
        out_specs=[VMEM] * len(out),
        out_shape=out,
        scratch_shapes=scratch,
        name=name,
    )(*(in_vmem(x) for x in args))


def whole_kernel(own_ref, near_ref, far_ref, both_ref, out_ref, whole_ref):
    for piece, piece_ref in enumerate((own_ref, near_ref, far_ref, both_ref)):
        whole_ref[block(piece, piece_ref.shape[0]), :] = piece_ref[...]
    out_ref[...] = whole_ref[...].T[0 : out_ref.shape[0], :]


def in_vmem(x):
    return pltpu.with_memory_space_constraint(x, pltpu.VMEM)


def exchanged(pieces, axis):
    return lax.all_to_all(pieces, axis, 0, 0, tiled=True)


def to_everyone(shard, peers):
    return jnp.broadcast_to(shard[None], (peers, *shard.shape))


def swapped(x, core, across):
    cores, chips = lax.axis_size("core"), lax.axis_size("x")
    pairs = []
    for c in range(cores):
        for i in range(chips):
            to = (c ^ core) * chips + (i ^ across)
            pairs.append((c * chips + i, to))
    return lax.ppermute(x, ("core", "x"), pairs)


def along(x, mask):
    chips = lax.axis_size("z")
    return lax.ppermute(x, "z", [(chip, chip ^ mask) for chip in range(chips)])


def four_kernel(own_ref, near_ref, next_ref, far_ref, out_ref):
    out_ref[...] = (own_ref[...] + near_ref[...]) + (far_ref[...] + next_ref[...])


def all_summed(keep, give, dtype, scale, held):
    total = keep + swapped(give, 1, 0)
    (total,) = call(
        four_kernel, "four", [pltpu.VMEM(keep.shape, jnp.float32)],
        (total, along(total, 1), along(total, 7), along(total, 6)),
    )
    total = ((total + along(total, 2)) * scale).astype(dtype)
    total, held = lax.optimization_barrier((total, held))
    return (total, swapped(total, 1, 0), swapped(total, 0, 1), swapped(total, 1, 1)), held


def local(data, shared_start):
    frames = data.shape[1]
    features = shared_start.shape[0]
    peers = lax.axis_size(("y", "x"))
    subjects = data.shape[0] * lax.axis_size(("z", "core"))
    size = padded(frames)
    packed, shared = packed_grams(data, shared_start.T, size)
    share = jnp.sum(exchanged(packed.reshape(peers, size // peers, size), ("y", "x")), axis=0)
    packed = exchanged(to_everyone(share, peers), ("y", "x")).reshape(size, size)
    blocks = [pltpu.VMEM((features // 4, size), jnp.float32)] * 2
    crosses = pltpu.VMEM((2, features, size), jnp.float32)
    squares = pltpu.VMEM((2, features, features), jnp.float32)
    keep, give = call(
        functools.partial(refit_kernel, frames), "refits", blocks, (packed, shared),
        [crosses, squares],
    )
    pieces, packed = all_summed(keep, give, jnp.bfloat16, 1.0 / subjects, packed)
    (parts,) = call(
        functools.partial(unpack_kernel, frames), "unpack",
        [pltpu.VMEM((2, 3, size, size), jnp.bfloat16)], (packed,),
    )
    keep, give, *state = call(
        last_kernel, "refits_last",
        [*blocks, crosses, squares, pltpu.VMEM((2, 8, LANES), jnp.float32)],
        (parts, *pieces), [pltpu.VMEM((features, size), jnp.bfloat16)],
    )
    pieces, state = all_summed(keep, give, jnp.float32, 1.0 / subjects, state)
    (projections,) = call(
        project_kernel, "project",
        [jax.ShapeDtypeStruct((2, frames, features), jnp.float32)], state,
    )
    (response,) = call(
        whole_kernel, "whole", [jax.ShapeDtypeStruct((frames, features), jnp.float32)], pieces,
        [pltpu.VMEM((features, size), jnp.float32)],
    )
    return (jnp.swapaxes(projections, 1, 2), response.T)


def solution(mesh):
    sizes = dict(mesh.shape)
    cores, across = 2, 4
    shape = (sizes["subj"] // cores, cores, sizes["vox"] // across, across)
    chips = Mesh(mesh.devices.reshape(shape), ("z", "core", "y", "x"))
    placed = (P(("z", "core"), None, ("y", "x")), P())
    return jax.shard_map(
        local,
        mesh=chips,
        in_specs=placed,
        out_specs=(P(("z", "core"), None, None), P()),
        check_vma=False,
    )
```

```python
import functools

import jax
import jax.numpy as jnp
from jax import lax
from jax.experimental import pallas as pl
from jax.experimental.pallas import tpu as pltpu
from jax.sharding import Mesh, PartitionSpec as P

ITERS = 3
LANES = 128
VMEM = pl.BlockSpec(memory_space=pltpu.VMEM)


def padded(frames):
    return -(-frames // (2 * LANES)) * 2 * LANES


def positions(size):
    rows = lax.broadcasted_iota(jnp.int32, (size, size), 0)
    cols = lax.broadcasted_iota(jnp.int32, (size, size), 1)
    return rows, cols


def gram_kernel(data_ref, start_ref, packed_ref, shared_ref, sums_ref):
    frames = data_ref.shape[1]

    @pl.when(pl.program_id(0) == 0)
    def _():
        shared_ref[...] = jnp.zeros_like(shared_ref)
        shared_ref[:, 0:frames] = start_ref[...].T
        packed_ref[...] = jnp.zeros_like(packed_ref)
        for subject in range(2):
            block = data_ref[subject]
            sums_ref[subject] = product(block, block, ((1,), (1,)))

    @pl.when(pl.program_id(0) == 1)
    def _():
        first, second = (
            sums_ref[subject] + product(data_ref[subject], data_ref[subject], ((1,), (1,)))
            for subject in range(2)
        )
        rows, cols = positions(frames)
        packed_ref[0:frames, 0:frames] = jnp.where(rows >= cols, first, second)
        packed_ref[0:frames, frames : frames + 1] = jnp.sum(
            jnp.where(rows == cols, second, 0.0), axis=1, keepdims=True
        )


def packed_grams(data, start, size):
    subjects, frames, voxels = data.shape
    features = start.shape[1]
    return pl.pallas_call(
        gram_kernel,
        grid=(2,),
        in_specs=[pl.BlockSpec((subjects, frames, voxels // 2), lambda i: (0, 0, i)), VMEM],
        out_specs=[VMEM, VMEM],
        out_shape=[
            pltpu.VMEM((size, size), jnp.float32),
            pltpu.VMEM((features, size), jnp.bfloat16),
        ],
        scratch_shapes=[pltpu.VMEM((subjects, frames, frames), jnp.float32)],
        name="grams",
    )(data, start)


def parts_of(x, count):
    parts = []
    for part in range(count):
        parts.append(x.astype(jnp.bfloat16))
        if part < count - 1:
            x = x - parts[-1].astype(jnp.float32)
    return parts


def product(a, b, dims=((1,), (0,))):
    return lax.dot_general(a, b, (dims, ((), ())), preferred_element_type=jnp.float32)


def halves(matrices):
    return [parts_of(matrix, 2) for matrix in matrices]


def times(a, b):
    high, low = b
    wide = jnp.concatenate([high, low], axis=1)
    out = product(jnp.concatenate(a, axis=1), jnp.concatenate([wide, wide], axis=0))
    return out[:, : high.shape[1]] + out[:, high.shape[1] :]


def unpacked(packed, frames):
    rows, cols = positions(packed.shape[0])
    diagonal = packed[:, frames : frames + 1]
    packed = jnp.where(cols < frames, packed, 0.0)
    flipped = packed.T
    return (
        jnp.where(rows >= cols, packed, flipped),
        jnp.where(rows == cols, diagonal, jnp.where(rows < cols, packed, flipped)),
    )


def refit(grams, shared, exact):
    crossed = [sum(product(shared, part) for part in parts) for parts in grams]
    wide = shared.astype(jnp.float32)
    squares = [jnp.sum(cross * wide) + 1e-06 for cross in crossed]
    split = [parts_of(cross, 3 if exact else 2) for cross in crossed]
    both = [product(shared, jnp.concatenate(parts[:2], axis=0), ((1,), (1,))) for parts in split]
    features = shared.shape[0]
    firsts = [pair[:, :features] + pair[:, features:] for pair in both]
    if exact:
        lows = [product(shared, parts[2], ((1,), (1,))) for parts in split]
        firsts = [first + low for first, low in zip(firsts, lows)]
    current = [first * (1.0 / square) for first, square in zip(firsts, squares)]
    taken, gain = None, 1.0
    for step in range(ITERS - 1):
        parts = halves(current)
        squared = [times(part, part) for part in parts]
        if step > 0:
            moved = [times(own, part) for own, part in zip(halves(taken), parts)]
        half = [1.5 * x - 0.5 * y for x, y in zip(current, squared)]
        cubed = [times(own, part) for own, part in zip(halves(half), parts)]
        if step > 0:
            taken = [1.5 * d + 0.5 * gain * x - 0.5 * y for d, x, y in zip(taken, current, moved)]
        else:
            taken = [0.5 * gain * x for x in current]
        gain *= 1.5
        current = [1.5 * x - 0.5 * y for x, y in zip(half, cubed)]
    moved = [against(own, part) for own, part in zip(halves(taken), split)]
    before = [gain * cross - part for cross, part in zip(crossed, moved)]
    return before, current, [1.0 / jnp.sqrt(square) for square in squares]


def against(a, b):
    high, low = b[:2]
    stacked = jnp.concatenate([high, high], axis=0)
    return product(jnp.concatenate(a, axis=1), stacked) + product(a[0], low)


def shares(keep_ref, give_ref, before_ref, current_ref, before, scales):
    width = keep_ref.shape[0]
    ahead, factor = [], []
    for piece in range(2):
        place = block(piece, width)
        ahead.append(sum(1.5 * scale * before_ref[s, place, :] for s, scale in enumerate(scales)))
        factor.append(
            jnp.concatenate(
                [0.5 * scale * current_ref[s, place, :] for s, scale in enumerate(scales)], axis=1
            )
        )
    high, low = parts_of(jnp.concatenate(factor, axis=0), 2)
    split = halves(before)
    upper = jnp.concatenate([parts[0] for parts in split], axis=0)
    lower = jnp.concatenate([parts[1] for parts in split], axis=0)
    moved = product(high, upper) + product(high, lower) + product(low, upper)
    keep_ref[...] = ahead[0] - moved[:width]
    give_ref[...] = ahead[1] - moved[width:]


def finish(grams, shared, exact, keep_ref, give_ref, before_ref, current_ref):
    before, current, scales = refit(grams, shared, exact)
    for subject in range(2):
        before_ref[subject] = before[subject]
        current_ref[subject] = current[subject]
    shares(keep_ref, give_ref, before_ref, current_ref, before, scales)
    return scales


def refit_kernel(frames, packed_ref, shared_ref, *refs):
    grams = [parts_of(gram, 3) for gram in unpacked(packed_ref[...], frames)]
    finish(grams, shared_ref[...], True, *refs)


def unpack_kernel(frames, packed_ref, parts_ref):
    for subject, gram in enumerate(unpacked(packed_ref[...], frames)):
        for part, half in enumerate(parts_of(gram, 3)):
            parts_ref[subject, part] = half


def last_kernel(parts_ref, own_ref, near_ref, *refs):
    *refs, scales_ref, shared_ref = refs
    for piece, piece_ref in enumerate((own_ref, near_ref)):
        shared_ref[block(piece, piece_ref.shape[0]), :] = piece_ref[...]
    grams = [[parts_ref[subject, part] for part in range(3)] for subject in range(2)]
    scales = finish(grams, shared_ref[...], False, *refs)
    for subject in range(2):
        scales_ref[subject] = jnp.full(scales_ref.shape[1:], scales[subject], jnp.float32)


def project_kernel(before_ref, current_ref, scales_ref, out_ref):
    for subject in range(2):
        before = before_ref[subject]
        moved = against(parts_of(current_ref[subject], 2), parts_of(before, 2))
        projected = (1.5 * before - 0.5 * moved) * scales_ref[subject, 0:1, 0:1]
        out_ref[subject] = projected.T[0 : out_ref.shape[1], :]


def block(piece, width):
    core = lax.axis_index("core")
    core = 1 - core if piece else core
    return pl.ds(pl.multiple_of(core * width, width), width)


def call(kernel, name, out, args, scratch=()):
    return pl.pallas_call(
        kernel,
        in_specs=[VMEM] * len(args),
        out_specs=[VMEM] * len(out),
        out_shape=out,
        scratch_shapes=scratch,
        name=name,
    )(*(in_vmem(x) for x in args))


def whole_kernel(own_ref, near_ref, out_ref, whole_ref):
    for piece, piece_ref in enumerate((own_ref, near_ref)):
        whole_ref[block(piece, piece_ref.shape[0]), :] = piece_ref[...]
    out_ref[...] = whole_ref[...].T[0 : out_ref.shape[0], :]


def in_vmem(x):
    return pltpu.with_memory_space_constraint(x, pltpu.VMEM)


def exchanged(pieces, axis):
    return lax.all_to_all(pieces, axis, 0, 0, tiled=True)


def to_everyone(shard, peers):
    return jnp.broadcast_to(shard[None], (peers, *shard.shape))


def swapped(x):
    return lax.ppermute(x, "core", [(0, 1), (1, 0)])


def along(x, mask):
    chips = lax.axis_size("z")
    return lax.ppermute(x, "z", [(chip, chip ^ mask) for chip in range(chips)])


def four_kernel(own_ref, near_ref, next_ref, far_ref, out_ref):
    out_ref[...] = (own_ref[...] + near_ref[...]) + (far_ref[...] + next_ref[...])


def all_summed(keep, give, dtype, scale, held):
    total = keep + swapped(give)
    (total,) = call(
        four_kernel, "four", [pltpu.VMEM(keep.shape, jnp.float32)],
        (total, along(total, 1), along(total, 7), along(total, 6)),
    )
    total = ((total + along(total, 2)) * scale).astype(dtype)
    total, held = lax.optimization_barrier((total, held))
    return (total, swapped(total)), held


def local(data, shared_start):
    frames = data.shape[1]
    features = shared_start.shape[0]
    peers = lax.axis_size(("y", "x"))
    subjects = data.shape[0] * lax.axis_size(("z", "core"))
    size = padded(frames)
    packed, shared = packed_grams(data, shared_start.T, size)
    share = jnp.sum(exchanged(packed.reshape(peers, size // peers, size), ("y", "x")), axis=0)
    packed = exchanged(to_everyone(share, peers), ("y", "x")).reshape(size, size)
    blocks = [pltpu.VMEM((features // 2, size), jnp.float32)] * 2
    crosses = pltpu.VMEM((2, features, size), jnp.float32)
    squares = pltpu.VMEM((2, features, features), jnp.float32)
    keep, give = call(
        functools.partial(refit_kernel, frames), "refits", blocks, (packed, shared),
        [crosses, squares],
    )
    pieces, packed = all_summed(keep, give, jnp.bfloat16, 1.0 / subjects, packed)
    (parts,) = call(
        functools.partial(unpack_kernel, frames), "unpack",
        [pltpu.VMEM((2, 3, size, size), jnp.bfloat16)], (packed,),
    )
    keep, give, *state = call(
        last_kernel, "refits_last",
        [*blocks, crosses, squares, pltpu.VMEM((2, 8, LANES), jnp.float32)],
        (parts, *pieces), [pltpu.VMEM((features, size), jnp.bfloat16)],
    )
    pieces, state = all_summed(keep, give, jnp.float32, 1.0 / subjects, state)
    (projections,) = call(
        project_kernel, "project",
        [jax.ShapeDtypeStruct((2, frames, features), jnp.float32)], state,
    )
    (response,) = call(
        whole_kernel, "whole", [jax.ShapeDtypeStruct((frames, features), jnp.float32)], pieces,
        [pltpu.VMEM((features, size), jnp.float32)],
    )
    return (jnp.swapaxes(projections, 1, 2), response.T)


def solution(mesh):
    sizes = dict(mesh.shape)
    cores, across = 2, 4
    shape = (sizes["subj"] // cores, cores, sizes["vox"] // across, across)
    chips = Mesh(mesh.devices.reshape(shape), ("z", "core", "y", "x"))
    placed = (P(("z", "core"), None, ("y", "x")), P())
    return jax.shard_map(
        local,
        mesh=chips,
        in_specs=placed,
        out_specs=(P(("z", "core"), None, None), P()),
        check_vma=False,
    )
```

```python
import functools

import jax
import jax.numpy as jnp
from jax import lax
from jax.experimental import pallas as pl
from jax.experimental.pallas import tpu as pltpu
from jax.sharding import Mesh, PartitionSpec as P

ITERS = 3
LANES = 128
VMEM = pl.BlockSpec(memory_space=pltpu.VMEM)


def padded(frames):
    return -(-frames // (2 * LANES)) * 2 * LANES


def positions(size):
    rows = lax.broadcasted_iota(jnp.int32, (size, size), 0)
    cols = lax.broadcasted_iota(jnp.int32, (size, size), 1)
    return rows, cols


def gram_kernel(data_ref, start_ref, packed_ref, shared_ref, sums_ref):
    frames = data_ref.shape[1]

    @pl.when(pl.program_id(0) == 0)
    def _():
        shared_ref[...] = jnp.zeros_like(shared_ref)
        shared_ref[:, 0:frames] = start_ref[...].T
        packed_ref[...] = jnp.zeros_like(packed_ref)
        for subject in range(2):
            block = data_ref[subject]
            sums_ref[subject] = product(block, block, ((1,), (1,)))

    @pl.when(pl.program_id(0) == 1)
    def _():
        first, second = (
            sums_ref[subject] + product(data_ref[subject], data_ref[subject], ((1,), (1,)))
            for subject in range(2)
        )
        rows, cols = positions(frames)
        packed_ref[0:frames, 0:frames] = jnp.where(rows >= cols, first, second)
        packed_ref[0:frames, frames : frames + 1] = jnp.sum(
            jnp.where(rows == cols, second, 0.0), axis=1, keepdims=True
        )


def packed_grams(data, start, size):
    subjects, frames, voxels = data.shape
    features = start.shape[1]
    return pl.pallas_call(
        gram_kernel,
        grid=(2,),
        in_specs=[pl.BlockSpec((subjects, frames, voxels // 2), lambda i: (0, 0, i)), VMEM],
        out_specs=[VMEM, VMEM],
        out_shape=[
            pltpu.VMEM((size, size), jnp.float32),
            pltpu.VMEM((features, size), jnp.bfloat16),
        ],
        scratch_shapes=[pltpu.VMEM((subjects, frames, frames), jnp.float32)],
        name="grams",
    )(data, start)


def parts_of(x, count):
    parts = []
    for part in range(count):
        parts.append(x.astype(jnp.bfloat16))
        if part < count - 1:
            x = x - parts[-1].astype(jnp.float32)
    return parts


def product(a, b, dims=((1,), (0,))):
    return lax.dot_general(a, b, (dims, ((), ())), preferred_element_type=jnp.float32)


def halves(matrices):
    return [parts_of(matrix, 2) for matrix in matrices]


def times(a, b):
    high, low = b
    wide = jnp.concatenate([high, low], axis=1)
    out = product(jnp.concatenate(a, axis=1), jnp.concatenate([wide, wide], axis=0))
    return out[:, : high.shape[1]] + out[:, high.shape[1] :]


def unpacked(packed, frames):
    rows, cols = positions(packed.shape[0])
    diagonal = packed[:, frames : frames + 1]
    packed = jnp.where(cols < frames, packed, 0.0)
    flipped = packed.T
    return (
        jnp.where(rows >= cols, packed, flipped),
        jnp.where(rows == cols, diagonal, jnp.where(rows < cols, packed, flipped)),
    )


def refit(grams, shared, exact):
    crossed = [sum(product(shared, part) for part in parts) for parts in grams]
    wide = shared.astype(jnp.float32)
    squares = [jnp.sum(cross * wide) + 1e-06 for cross in crossed]
    split = [parts_of(cross, 3 if exact else 2) for cross in crossed]
    both = [product(shared, jnp.concatenate(parts[:2], axis=0), ((1,), (1,))) for parts in split]
    features = shared.shape[0]
    firsts = [pair[:, :features] + pair[:, features:] for pair in both]
    if exact:
        lows = [product(shared, parts[2], ((1,), (1,))) for parts in split]
        firsts = [first + low for first, low in zip(firsts, lows)]
    current = [first * (1.0 / square) for first, square in zip(firsts, squares)]
    taken, gain = None, 1.0
    for step in range(ITERS - 1):
        parts = halves(current)
        squared = [times(part, part) for part in parts]
        if step > 0:
            moved = [times(own, part) for own, part in zip(halves(taken), parts)]
        half = [1.5 * x - 0.5 * y for x, y in zip(current, squared)]
        cubed = [times(own, part) for own, part in zip(halves(half), parts)]
        if step > 0:
            taken = [1.5 * d + 0.5 * gain * x - 0.5 * y for d, x, y in zip(taken, current, moved)]
        else:
            taken = [0.5 * gain * x for x in current]
        gain *= 1.5
        current = [1.5 * x - 0.5 * y for x, y in zip(half, cubed)]
    moved = [against(own, part) for own, part in zip(halves(taken), split)]
    before = [gain * cross - part for cross, part in zip(crossed, moved)]
    return before, current, [1.0 / jnp.sqrt(square) for square in squares]


def against(a, b):
    high, low = b[:2]
    stacked = jnp.concatenate([high, high], axis=0)
    return product(jnp.concatenate(a, axis=1), stacked) + product(a[0], low)


def shares(keep_ref, give_ref, before_ref, current_ref, before, scales):
    width = keep_ref.shape[0]
    ahead, factor = [], []
    for piece in range(2):
        place = block(piece, width)
        ahead.append(sum(1.5 * scale * before_ref[s, place, :] for s, scale in enumerate(scales)))
        factor.append(
            jnp.concatenate(
                [0.5 * scale * current_ref[s, place, :] for s, scale in enumerate(scales)], axis=1
            )
        )
    high, low = parts_of(jnp.concatenate(factor, axis=0), 2)
    split = halves(before)
    upper = jnp.concatenate([parts[0] for parts in split], axis=0)
    lower = jnp.concatenate([parts[1] for parts in split], axis=0)
    moved = product(high, upper) + product(high, lower) + product(low, upper)
    keep_ref[...] = ahead[0] - moved[:width]
    give_ref[...] = ahead[1] - moved[width:]


def finish(grams, shared, exact, keep_ref, give_ref, before_ref, current_ref):
    before, current, scales = refit(grams, shared, exact)
    for subject in range(2):
        before_ref[subject] = before[subject]
        current_ref[subject] = current[subject]
    shares(keep_ref, give_ref, before_ref, current_ref, before, scales)
    return scales


def refit_kernel(frames, packed_ref, shared_ref, *refs):
    grams = [parts_of(gram, 3) for gram in unpacked(packed_ref[...], frames)]
    finish(grams, shared_ref[...], True, *refs)


def unpack_kernel(frames, packed_ref, parts_ref):
    for subject, gram in enumerate(unpacked(packed_ref[...], frames)):
        for part, half in enumerate(parts_of(gram, 3)):
            parts_ref[subject, part] = half


def last_kernel(parts_ref, own_ref, near_ref, *refs):
    *refs, scales_ref, shared_ref = refs
    for piece, piece_ref in enumerate((own_ref, near_ref)):
        shared_ref[block(piece, piece_ref.shape[0]), :] = piece_ref[...]
    grams = [[parts_ref[subject, part] for part in range(3)] for subject in range(2)]
    scales = finish(grams, shared_ref[...], False, *refs)
    for subject in range(2):
        scales_ref[subject] = jnp.full(scales_ref.shape[1:], scales[subject], jnp.float32)


def project_kernel(before_ref, current_ref, scales_ref, out_ref):
    for subject in range(2):
        before = before_ref[subject]
        moved = against(parts_of(current_ref[subject], 2), parts_of(before, 2))
        projected = (1.5 * before - 0.5 * moved) * scales_ref[subject, 0:1, 0:1]
        out_ref[subject] = projected.T[0 : out_ref.shape[1], :]


def block(piece, width):
    core = lax.axis_index("core")
    core = 1 - core if piece else core
    return pl.ds(pl.multiple_of(core * width, width), width)


def call(kernel, name, out, args, scratch=()):
    return pl.pallas_call(
        kernel,
        in_specs=[VMEM] * len(args),
        out_specs=[VMEM] * len(out),
        out_shape=out,
        scratch_shapes=scratch,
        name=name,
    )(*(in_vmem(x) for x in args))


def whole_kernel(own_ref, near_ref, out_ref, whole_ref):
    for piece, piece_ref in enumerate((own_ref, near_ref)):
        whole_ref[block(piece, piece_ref.shape[0]), :] = piece_ref[...]
    out_ref[...] = whole_ref[...].T[0 : out_ref.shape[0], :]


def in_vmem(x):
    return pltpu.with_memory_space_constraint(x, pltpu.VMEM)


def exchanged(pieces, axis):
    return lax.all_to_all(pieces, axis, 0, 0, tiled=True)


def to_everyone(shard, peers):
    return jnp.broadcast_to(shard[None], (peers, *shard.shape))


def swapped(x):
    return lax.ppermute(x, "core", [(0, 1), (1, 0)])


def along(x, mask):
    chips = lax.axis_size("z")
    return lax.ppermute(x, "z", [(chip, chip ^ mask) for chip in range(chips)])


def four_kernel(own_ref, near_ref, far_ref, next_ref, out_ref):
    out_ref[...] = (own_ref[...] + near_ref[...]) + (far_ref[...] + next_ref[...])


def all_summed(keep, give, dtype, scale, held):
    total = keep + swapped(give)
    (total,) = call(
        four_kernel, "four", [pltpu.VMEM(keep.shape, jnp.float32)],
        (total, along(total, 1), along(total, 6), along(total, 7)),
    )
    total = ((total + along(total, 2)) * scale).astype(dtype)
    total, held = lax.optimization_barrier((total, held))
    return (total, swapped(total)), held


def local(data, shared_start):
    frames = data.shape[1]
    features = shared_start.shape[0]
    peers = lax.axis_size(("y", "x"))
    subjects = data.shape[0] * lax.axis_size(("z", "core"))
    size = padded(frames)
    packed, shared = packed_grams(data, shared_start.T, size)
    share = jnp.sum(exchanged(packed.reshape(peers, size // peers, size), ("y", "x")), axis=0)
    packed = exchanged(to_everyone(share, peers), ("y", "x")).reshape(size, size)
    blocks = [pltpu.VMEM((features // 2, size), jnp.float32)] * 2
    crosses = pltpu.VMEM((2, features, size), jnp.float32)
    squares = pltpu.VMEM((2, features, features), jnp.float32)
    keep, give = call(
        functools.partial(refit_kernel, frames), "refits", blocks, (packed, shared),
        [crosses, squares],
    )
    pieces, packed = all_summed(keep, give, jnp.bfloat16, 1.0 / subjects, packed)
    (parts,) = call(
        functools.partial(unpack_kernel, frames), "unpack",
        [pltpu.VMEM((2, 3, size, size), jnp.bfloat16)], (packed,),
    )
    keep, give, *state = call(
        last_kernel, "refits_last",
        [*blocks, crosses, squares, pltpu.VMEM((2, 8, LANES), jnp.float32)],
        (parts, *pieces), [pltpu.VMEM((features, size), jnp.bfloat16)],
    )
    pieces, state = all_summed(keep, give, jnp.float32, 1.0 / subjects, state)
    (projections,) = call(
        project_kernel, "project",
        [jax.ShapeDtypeStruct((2, frames, features), jnp.float32)], state,
    )
    (response,) = call(
        whole_kernel, "whole", [jax.ShapeDtypeStruct((frames, features), jnp.float32)], pieces,
        [pltpu.VMEM((features, size), jnp.float32)],
    )
    return (jnp.swapaxes(projections, 1, 2), response.T)


def solution(mesh):
    sizes = dict(mesh.shape)
    cores, across = 2, 4
    shape = (sizes["subj"] // cores, cores, sizes["vox"] // across, across)
    chips = Mesh(mesh.devices.reshape(shape), ("z", "core", "y", "x"))
    placed = (P(("z", "core"), None, ("y", "x")), P())
    return jax.shard_map(
        local,
        mesh=chips,
        in_specs=placed,
        out_specs=(P(("z", "core"), None, None), P()),
        check_vma=False,
    )
```
